128 devices in a mesh: seq: 16 (over x, y), head: 8 (over z, core).
Axes of the slice: x: 4, y: 4, z: 4, core: 2. Of those that a mesh axis runs over, the one named last changes fastest.
Arguments:
- query: bfloat16 [16384, 7168], P(('seq', 'head')), may hold values from -16 to 16
- key: bfloat16 [16384, 7168], P(('seq', 'head')), may hold values from -16 to 16
- value: bfloat16 [16384, 7168], P(('seq', 'head')), may hold values from -8 to 8
- exponent: int32 [64], replicated, may hold values from 1 to 64, as said below
Outputs:
- attended: bfloat16 [16384, 7168], P(('seq', 'head'))
The draws below stay inside these ranges and needn't reach their ends.
Inputs may be any that keep to these rules, and one draw needn't show every extreme that they name: Head h (counted from 0) has an exponent within 6 of h + 1; head 0 has 1 and the last head has 64.
All inputs are finite; a program needn't handle non-finite values.
Results may differ from the reference program's by a relative error of at most 0.0033.
Values may be sent and summed in bfloat16 or wider, within the bound.
A program may use at most 128 MiB of HBM per device.

```python
import jax
import jax.numpy as jnp
from jax import lax

HEADS = 64
HS = 112
D = 7168
BLOCK = 128
MIN_BAND = 16
MAX_BAND = 40
TOKENS = 16384


def exponent_draw(key):
    jitter = jax.random.randint(jax.random.fold_in(key, 301), (HEADS,), -6, 7)
    ranks = jnp.arange(HEADS, dtype=jnp.int32)
    drawn = jnp.clip(ranks + 1 + jitter, 1, HEADS)
    drawn = jnp.where(ranks == 0, 1, drawn)
    drawn = jnp.where(ranks == HEADS - 1, HEADS, drawn)
    return drawn.astype(jnp.int32)


def paired_draw(key):
    first_key = jax.random.fold_in(key, 101)
    second_key = jax.random.fold_in(key, 102)
    queries = jnp.clip(jax.random.normal(first_key, (TOKENS, D), jnp.float32), -6.0, 6.0)
    keys_drawn = jnp.clip(jax.random.normal(second_key, (TOKENS, D), jnp.float32), -6.0, 6.0)
    return (queries, keys_drawn)


def draw_query(key, part):
    return paired_draw(key)[0].astype(jnp.bfloat16)


def draw_key(key, part):
    return paired_draw(key)[1].astype(jnp.bfloat16)


def draw_value(key, part):
    noise_key = jax.random.fold_in(key, 201)
    offset_key = jax.random.fold_in(key, 202)
    offsets = jax.random.uniform(offset_key, (TOKENS // BLOCK, D), jnp.float32, -2.0, 2.0)
    offsets = jnp.repeat(offsets, BLOCK, axis=0)
    noise = jnp.clip(jax.random.normal(noise_key, (TOKENS, D), jnp.float32), -6.0, 6.0)
    drawn = noise + offsets
    return drawn.astype(jnp.bfloat16)


def draw_exponent(key, part):
    return exponent_draw(key)


def setup_inputs(seed: int = 0) -> dict:
    splits = jax.random.split(jax.random.key(seed), 5)
    return {
        "query": draw_query(jax.random.fold_in(splits[4], 71), 0),
        "key": draw_key(jax.random.fold_in(splits[4], 71), 0),
        "value": draw_value(jax.random.fold_in(splits[4], 71), 0),
        "exponent": draw_exponent(jax.random.fold_in(splits[4], 71), 0),
    }


def reference(query, key, value, exponent):
    slopes = jnp.exp2(-12.0 * exponent.astype(jnp.float32) / HEADS)
    bands = MIN_BAND + ((exponent.astype(jnp.int32) - 1) * (MAX_BAND - MIN_BAND)) // (HEADS - 1)
    query_rows = min(512, TOKENS)
    window_rows = MAX_BAND * BLOCK
    factor = HS ** -0.5
    heads_query = query.reshape(TOKENS, HEADS, HS).transpose(1, 0, 2)
    padding = jnp.zeros((HEADS, window_rows, HS), key.dtype)
    heads_key = jnp.concatenate([padding, key.reshape(TOKENS, HEADS, HS).transpose(1, 0, 2)], axis=1)
    heads_value = jnp.concatenate([padding, value.reshape(TOKENS, HEADS, HS).transpose(1, 0, 2)], axis=1)

    def one_head(packed):
        query_head, key_head, value_head, head_slope, head_band = packed

        def one_block(block_id):
            first = (block_id * query_rows).astype(jnp.int32)
            query_block = lax.dynamic_slice_in_dim(query_head, first, query_rows, 0)
            key_window = lax.dynamic_slice_in_dim(key_head, first, window_rows + query_rows, 0)
            value_window = lax.dynamic_slice_in_dim(value_head, first, window_rows + query_rows, 0)
            query_pos = first + jnp.arange(query_rows, dtype=jnp.int32)
            key_pos = first - window_rows + jnp.arange(window_rows + query_rows, dtype=jnp.int32)
            distance = query_pos[:, None] - key_pos[None, :]
            scores = jnp.dot(query_block, key_window.T, preferred_element_type=jnp.float32) * factor
            scores = scores - head_slope * distance.astype(jnp.float32)
            live = (key_pos[None, :] >= 0) & (distance >= 0) & (query_pos[:, None] // BLOCK - key_pos[None, :] // BLOCK < head_band)
            scores = jnp.where(live, scores, -1.0e30)
            highest = jnp.max(scores, axis=1, keepdims=True)
            weights = jnp.where(live, jnp.exp(scores - highest), 0.0)
            weight_sum = jnp.sum(weights, axis=1, keepdims=True)
            mixed = jnp.dot(weights.astype(jnp.bfloat16), value_window, preferred_element_type=jnp.float32)
            return (mixed / weight_sum).astype(jnp.bfloat16)

        blocks = lax.map(one_block, jnp.arange(TOKENS // query_rows, dtype=jnp.int32))
        return blocks.reshape(TOKENS, HS)

    result = lax.map(one_head, (heads_query, heads_key, heads_value, slopes, bands))
    return result.transpose(1, 0, 2).reshape(TOKENS, D)
```

```python
import functools

import jax
import jax.numpy as jnp
from jax import lax
from jax.experimental import pallas as pl
from jax.experimental.pallas import tpu as pltpu
from jax.sharding import PartitionSpec as P

BLOCK = 128
MIN_BAND = 16
MAX_BAND = 40
HEADS = 64
HS = 112
D = HEADS * HS
PLANE = 32
HALO = 40
MESH = pl.DeviceIdType.MESH
LOG2E = 1.4426950408889634


def coords():
    seq = lax.axis_index("seq")
    head = lax.axis_index("head")
    x = seq // 4
    p = (seq % 4) * 8 + head
    return x, p


def device_of(x, p):
    return (x * 4 + p // 8, p % 8)


def most_band(slot, p):
    if slot == 0:
        return MIN_BAND + (p + 6) * 24 // 63
    return MIN_BAND + (69 - p) * 24 // 63


def head_of(slot, p):
    return p if slot == 0 else HEADS - 1 - p


def head_rows(slot, p):
    return pl.ds(pl.multiple_of(head_of(slot, p) * HS, 16), HS)


def enter(x, p):
    barrier = pltpu.get_barrier_semaphore()

    def greet(d, carry):
        pl.semaphore_signal(
            barrier, inc=1, device_id=device_of(x, (p + d) % PLANE), device_id_type=MESH
        )
        return carry

    lax.fori_loop(1, PLANE, greet, 0)
    for d in range(1, 4):
        pl.semaphore_signal(barrier, inc=1, device_id=device_of((x + d) % 4, p), device_id_type=MESH)
    pl.semaphore_wait(barrier, PLANE - 1 + 3)


def dispatch_kernel(
    q_ref, k_ref, v_ref, group, halo, turned, send, recv, halo_send, halo_recv, far_send, own
):
    x, p = coords()
    eye = (
        lax.broadcasted_iota(jnp.int32, (BLOCK, BLOCK), 0)
        == lax.broadcasted_iota(jnp.int32, (BLOCK, BLOCK), 1)
    ).astype(jnp.bfloat16)

    def turn(step, carry):
        for part in range(4):
            at = pl.multiple_of((step * 4 + part) * BLOCK, BLOCK)
            for c, ref in enumerate((q_ref, k_ref, v_ref)):
                tile = ref[:, pl.ds(at, BLOCK)]
                turned[c, pl.ds(at, BLOCK), :] = lax.dot_general(
                    eye, tile, (((1,), (1,)), ((), ())), preferred_element_type=jnp.float32
                ).astype(jnp.bfloat16)
        return carry

    lax.fori_loop(0, D // BLOCK // 4, turn, 0)
    enter(x, p)

    def to_peer(d, slot):
        peer = (p + d) % PLANE
        return pltpu.make_async_remote_copy(
            src_ref=turned.at[:, head_rows(slot, peer), :],
            dst_ref=group.at[p, slot],
            send_sem=send.at[d, slot],
            recv_sem=recv.at[p, slot],
            device_id=device_of(x, peer),
            device_id_type=MESH,
        )

    def from_peer(j, slot):
        return pltpu.make_async_remote_copy(
            src_ref=turned.at[:, pl.ds(0, HS), :],
            dst_ref=group.at[j, slot],
            send_sem=send.at[0, slot],
            recv_sem=recv.at[j, slot],
            device_id=device_of(x, (p + 1) % PLANE),
            device_id_type=MESH,
        )

    def near(j, slot):
        return pltpu.make_async_remote_copy(
            src_ref=group.at[j, slot, pl.ds(1, 2)],
            dst_ref=halo.at[8 + j, slot],
            send_sem=halo_send.at[j, slot],
            recv_sem=halo_recv.at[8 + j, slot],
            device_id=device_of((x + 1) % 4, p),
            device_id_type=MESH,
        )

    def far(j):
        return pltpu.make_async_remote_copy(
            src_ref=group.at[j, 1, pl.ds(1, 2)],
            dst_ref=halo.at[j - 24, 1],
            send_sem=far_send.at[j - 24],
            recv_sem=halo_recv.at[j - 24, 1],
            device_id=device_of((x + 2) % 4, p),
            device_id_type=MESH,
        )

    def start_all(d, carry):
        for slot in range(2):
            to_peer(d, slot).start()
        return carry

    lax.fori_loop(1, PLANE, start_all, 0)
    own_copies = [
        pltpu.make_async_copy(
            turned.at[:, head_rows(slot, p), :], group.at[p, slot], own.at[slot]
        )
        for slot in range(2)
    ]
    for copy in own_copies:
        copy.start()

    def near_needed(j, slot):
        return (x < 3) & (j >= 33 - most_band(slot, p))

    def far_needed(j):
        return (x < 2) & (j >= 25) & (j >= 65 - most_band(1, p))

    def forward(j, slot):
        @pl.when(near_needed(j, slot))
        def _():
            near(j, slot).start()

        if slot == 1:

            @pl.when(far_needed(j))
            def _():
                far(j).start()

    for slot, copy in enumerate(own_copies):
        copy.wait()
        forward(p, slot)

    def take(d, carry):
        j = (p + PLANE - d) % PLANE
        for slot in range(2):
            from_peer(j, slot).wait_recv()
            forward(j, slot)
        return carry

    lax.fori_loop(1, PLANE, take, 0)

    def finish(d, carry):
        for slot in range(2):
            @pl.when(d > 0)
            def _():
                to_peer(d, slot).wait_send()

            @pl.when(near_needed(d, slot))
            def _():
                near(d, slot).wait_send()

            @pl.when((x > 0) & (d >= 33 - most_band(slot, p)))
            def _():
                near(d, slot).wait_recv()

        @pl.when(far_needed(d))
        def _():
            far(d).wait_send()

        @pl.when((x > 1) & (d >= 25) & (d >= 65 - most_band(1, p)))
        def _():
            far(d).wait_recv()

        return carry

    lax.fori_loop(0, PLANE, finish, 0)


def dispatch(query, key, value):
    return pl.pallas_call(
        dispatch_kernel,
        out_shape=(
            jax.ShapeDtypeStruct((PLANE, 2, 3, HS, BLOCK), jnp.bfloat16),
            jax.ShapeDtypeStruct((HALO, 2, 2, HS, BLOCK), jnp.bfloat16),
        ),
        in_specs=[pl.BlockSpec(memory_space=pltpu.VMEM)] * 3,
        out_specs=(pl.BlockSpec(memory_space=pl.ANY), pl.BlockSpec(memory_space=pl.ANY)),
        scratch_shapes=[
            pltpu.VMEM((3, D, BLOCK), jnp.bfloat16),
            pltpu.SemaphoreType.DMA((PLANE, 2)),
            pltpu.SemaphoreType.DMA((PLANE, 2)),
            pltpu.SemaphoreType.DMA((PLANE, 2)),
            pltpu.SemaphoreType.DMA((HALO, 2)),
            pltpu.SemaphoreType.DMA((8,)),
            pltpu.SemaphoreType.DMA((2,)),
        ],
        compiler_params=pltpu.CompilerParams(
            collective_id=0, has_side_effects=True, vmem_limit_bytes=40 << 20
        ),
        name="dispatch",
    )(query, key, value)


def attend_kernel(
    band_ref, where_ref, slope_ref, group, halo, out, keys, values, weight_rows, acc_a, acc_b
):
    slot = pl.program_id(0)
    step = pl.program_id(1)
    x = where_ref[0]
    band = band_ref[slot]
    factor = HS ** (-0.5)
    scale = factor * LOG2E

    @pl.when(step == 0)
    def _():
        eye = (
            lax.broadcasted_iota(jnp.int32, (BLOCK, BLOCK), 0)
            == lax.broadcasted_iota(jnp.int32, (BLOCK, BLOCK), 1)
        ).astype(jnp.bfloat16)
        row = lax.broadcasted_iota(jnp.int32, (16, BLOCK), 0)
        token = lax.broadcasted_iota(jnp.int32, (16, BLOCK), 1).astype(jnp.float32)
        ones = jnp.ones((16, BLOCK), jnp.bfloat16)

        def put(index, key_t, value_t):
            block = (index - HALO).astype(jnp.float32)
            extra = jnp.where(row < 3, block, jnp.where(row < 6, token, 0.0)).astype(jnp.bfloat16)
            whole = jnp.concatenate([key_t, extra], axis=0)
            at = pl.multiple_of(index * BLOCK, BLOCK)
            keys[pl.ds(at, BLOCK), :] = lax.dot_general(
                eye, whole, (((1,), (1,)), ((), ())), preferred_element_type=jnp.float32
            ).astype(jnp.bfloat16)
            values[:, pl.ds(at, BLOCK)] = jnp.concatenate([value_t, ones], axis=0)

        def put_halo(index, carry):
            live = (index - HALO >= -PLANE * x) & (index - HALO > -band)

            @pl.when(live)
            def _():
                put(index, halo[index, 0, 0], halo[index, 0, 1])

            @pl.when(jnp.logical_not(live))
            def _():
                nothing = jnp.zeros((HS, BLOCK), jnp.bfloat16)
                put(index, nothing, nothing)

            return carry

        lax.fori_loop(0, HALO, put_halo, 0)

        def put_group(index, carry):
            put(index + HALO, group[index, 0, 1], group[index, 0, 2])
            return carry

        lax.fori_loop(0, PLANE, put_group, 0)

        slope = slope_ref[0:1, :] * (BLOCK / factor)
        high = slope.astype(jnp.bfloat16).astype(jnp.float32)
        middle = (slope - high).astype(jnp.bfloat16).astype(jnp.float32)
        low = (slope - high - middle).astype(jnp.bfloat16).astype(jnp.float32)
        kind = row % 3
        parts = jnp.where(kind == 0, high, jnp.where(kind == 1, middle, low))
        parts = jnp.where(row < 3, parts, jnp.where(row < 6, parts * (1.0 / BLOCK), 0.0))
        weight_rows[...] = jnp.concatenate([parts, parts], axis=1).astype(jnp.bfloat16)

    def query_tile(first):
        pair = jnp.concatenate([group[first, 0, 0], group[first + 1, 0, 0]], axis=1)
        return jnp.concatenate([pair, weight_rows[...]], axis=0)

    def scores(first_block, count, query):
        at = pl.multiple_of((first_block + HALO) * BLOCK, BLOCK)
        return jnp.dot(
            keys[pl.ds(at, count * BLOCK), :], query, preferred_element_type=jnp.float32
        )

    def mix(first_block, count, weight):
        at = pl.multiple_of((first_block + HALO) * BLOCK, BLOCK)
        return jnp.dot(
            values[:, pl.ds(at, count * BLOCK)],
            weight.astype(jnp.bfloat16),
            preferred_element_type=jnp.float32,
        )

    firsts = (step * 4, step * 4 + 2)
    queries = [query_tile(first) for first in firsts]
    accs = (acc_a, acc_b)
    wide = 2 * BLOCK
    causal = lax.broadcasted_iota(jnp.int32, (wide, wide), 0) <= lax.broadcasted_iota(
        jnp.int32, (wide, wide), 1
    )
    tops = []
    for first, query, acc in zip(firsts, queries, accs):
        s = jnp.where(causal, scores(first, 2, query), -1e30)
        top = jnp.max(s, axis=0, keepdims=True)
        acc[...] = mix(first, 2, jnp.exp2((s - top) * scale))
        tops.append(top)

    def go(first, query, acc, top, start, live):
        s = scores(start, 4, query)
        if live is not None:
            s = jnp.where(live, s, -1e30)
        new = jnp.maximum(top, jnp.max(s, axis=0, keepdims=True))
        weight = jnp.exp2((s - new) * scale)
        shrink = jnp.exp2((top - new) * scale)
        acc[...] = acc[...] * shrink + mix(start, 4, weight)
        return new

    full = jnp.minimum(band - 2, step * 4 + PLANE * x) // 4

    def middle_step(n, tops):
        return tuple(
            go(first, query, acc, top, first - 4 * n - 4, None)
            for first, query, acc, top in zip(firsts, queries, accs, tops)
        )

    tops = lax.fori_loop(0, full, middle_step, tuple(tops))
    key_block = lax.broadcasted_iota(jnp.int32, (4 * BLOCK, wide), 0) // BLOCK
    query_block = lax.broadcasted_iota(jnp.int32, (4 * BLOCK, wide), 1) // BLOCK
    for part, (first, query, acc, top) in enumerate(zip(firsts, queries, accs, tops)):
        start = first - 4 * full - 4
        live = (key_block + start > query_block + (first - band)) & (
            key_block + start >= -PLANE * x
        )
        go(first, query, acc, top, start, live)
        result = (acc[0:HS, :] / acc[HS : HS + 1, :]).astype(jnp.bfloat16)
        out[2 * part, 0] = result[:, :BLOCK]
        out[2 * part + 1, 0] = result[:, BLOCK:]


def attend(bands, where, slopes, group, halo):
    return pl.pallas_call(
        attend_kernel,
        out_shape=jax.ShapeDtypeStruct((PLANE, 2, HS, BLOCK), jnp.bfloat16),
        grid_spec=pltpu.PrefetchScalarGridSpec(
            num_scalar_prefetch=2,
            grid=(2, PLANE // 4),
            in_specs=[
                pl.BlockSpec((None, 8, BLOCK), lambda i, j, *_: (i, 0, 0)),
                pl.BlockSpec((PLANE, 1, 3, HS, BLOCK), lambda i, j, *_: (0, i, 0, 0, 0)),
                pl.BlockSpec((HALO, 1, 2, HS, BLOCK), lambda i, j, *_: (0, i, 0, 0, 0)),
            ],
            out_specs=pl.BlockSpec((4, 1, HS, BLOCK), lambda i, j, *_: (j, i, 0, 0)),
            scratch_shapes=[
                pltpu.VMEM(((HALO + PLANE) * BLOCK, BLOCK), jnp.bfloat16),
                pltpu.VMEM((BLOCK, (HALO + PLANE) * BLOCK), jnp.bfloat16),
                pltpu.VMEM((16, 2 * BLOCK), jnp.bfloat16),
                pltpu.VMEM((BLOCK, 2 * BLOCK), jnp.float32),
                pltpu.VMEM((BLOCK, 2 * BLOCK), jnp.float32),
            ],
        ),
        compiler_params=pltpu.CompilerParams(
            dimension_semantics=("arbitrary", "arbitrary"), vmem_limit_bytes=50 << 20
        ),
        name="attend",
    )(bands, where, slopes, group, halo)


def combine_kernel(mixed, out, back, send, recv, own):
    x, p = coords()
    enter(x, p)

    def to_peer(d, slot):
        peer = (p + d) % PLANE
        return pltpu.make_async_remote_copy(
            src_ref=mixed.at[peer, slot],
            dst_ref=back.at[head_rows(slot, p), :],
            send_sem=send.at[d, slot],
            recv_sem=recv.at[p, slot],
            device_id=device_of(x, peer),
            device_id_type=MESH,
        )

    def from_peer(j, slot):
        return pltpu.make_async_remote_copy(
            src_ref=mixed.at[0, slot],
            dst_ref=back.at[head_rows(slot, j), :],
            send_sem=send.at[0, slot],
            recv_sem=recv.at[j, slot],
            device_id=device_of(x, (p + 1) % PLANE),
            device_id_type=MESH,
        )

    def start_all(d, carry):
        for slot in range(2):
            to_peer(d, slot).start()
        return carry

    lax.fori_loop(1, PLANE, start_all, 0)
    for slot in range(2):
        copy = pltpu.make_async_copy(
            mixed.at[p, slot], back.at[head_rows(slot, p), :], own.at[slot]
        )
        copy.start()
        copy.wait()

    def finish(d, carry):
        j = (p + PLANE - d) % PLANE
        for slot in range(2):
            from_peer(j, slot).wait_recv()
            to_peer(d, slot).wait_send()
        return carry

    lax.fori_loop(1, PLANE, finish, 0)
    eye = (
        lax.broadcasted_iota(jnp.int32, (BLOCK, BLOCK), 0)
        == lax.broadcasted_iota(jnp.int32, (BLOCK, BLOCK), 1)
    ).astype(jnp.bfloat16)

    def turn(step, carry):
        for part in range(4):
            at = pl.multiple_of((step * 4 + part) * BLOCK, BLOCK)
            out[:, pl.ds(at, BLOCK)] = lax.dot_general(
                eye, back[pl.ds(at, BLOCK), :], (((1,), (1,)), ((), ())),
                preferred_element_type=jnp.float32,
            ).astype(jnp.bfloat16)
        return carry

    lax.fori_loop(0, D // BLOCK // 4, turn, 0)


def combine(mixed):
    return pl.pallas_call(
        combine_kernel,
        out_shape=jax.ShapeDtypeStruct((BLOCK, D), jnp.bfloat16),
        in_specs=[pl.BlockSpec(memory_space=pltpu.VMEM)],
        out_specs=pl.BlockSpec(memory_space=pltpu.VMEM),
        scratch_shapes=[
            pltpu.VMEM((D, BLOCK), jnp.bfloat16),
            pltpu.SemaphoreType.DMA((PLANE, 2)),
            pltpu.SemaphoreType.DMA((PLANE, 2)),
            pltpu.SemaphoreType.DMA((2,)),
        ],
        compiler_params=pltpu.CompilerParams(
            collective_id=1, has_side_effects=True, vmem_limit_bytes=40 << 20
        ),
        name="combine",
    )(mixed)


def on_device(query, key, value, exponent):
    x, p = coords()
    heads = jnp.stack([p, HEADS - 1 - p])
    local = jnp.take(exponent, heads)
    bands = MIN_BAND + (local - 1) * (MAX_BAND - MIN_BAND) // (HEADS - 1)
    slopes = jnp.exp2(-12.0 * local.astype(jnp.float32) / HEADS)
    slopes = jnp.broadcast_to(slopes[:, None, None], (2, 8, BLOCK))
    group, halo = dispatch(query, key, value)
    mixed = attend(bands, x[None], slopes, group, halo)
    return combine(mixed)


def solution(mesh):
    return jax.shard_map(
        on_device,
        mesh=mesh,
        in_specs=(
            P(("seq", "head"), None),
            P(("seq", "head"), None),
            P(("seq", "head"), None),
            P(),
        ),
        out_specs=P(("seq", "head"), None),
        check_vma=False,
    )
```

```python
import functools

import jax
import jax.numpy as jnp
from jax import lax
from jax.experimental import pallas as pl
from jax.experimental.pallas import tpu as pltpu
from jax.sharding import PartitionSpec as P

BLOCK = 128
MIN_BAND = 16
MAX_BAND = 40
HEADS = 64
HS = 112
D = HEADS * HS
PLANE = 32
HALO = 40
MESH = pl.DeviceIdType.MESH
LOG2E = 1.4426950408889634
PARTS = (pl.ds(1, 2), pl.ds(0, 1))


def coords():
    seq = lax.axis_index("seq")
    head = lax.axis_index("head")
    x = seq // 4
    p = (seq % 4) * 8 + head
    return x, p


def device_of(x, p):
    return (x * 4 + p // 8, p % 8)


def most_band(slot, p):
    if slot == 0:
        return MIN_BAND + (p + 6) * 24 // 63
    return MIN_BAND + (69 - p) * 24 // 63


def head_of(slot, p):
    return p if slot == 0 else HEADS - 1 - p


def head_rows(slot, p):
    return pl.ds(pl.multiple_of(head_of(slot, p) * HS, 16), HS)


def enter(x, p):
    barrier = pltpu.get_barrier_semaphore()

    def greet(d, carry):
        pl.semaphore_signal(
            barrier, inc=1, device_id=device_of(x, (p + d) % PLANE), device_id_type=MESH
        )
        return carry

    lax.fori_loop(1, PLANE, greet, 0)
    for d in range(1, 4):
        pl.semaphore_signal(barrier, inc=1, device_id=device_of((x + d) % 4, p), device_id_type=MESH)
    pl.semaphore_wait(barrier, PLANE - 1 + 3)


def dispatch_kernel(
    q_ref, k_ref, v_ref, group, halo, turned, send, recv, halo_send, halo_recv, far_send, own
):
    x, p = coords()
    eye = (
        lax.broadcasted_iota(jnp.int32, (BLOCK, BLOCK), 0)
        == lax.broadcasted_iota(jnp.int32, (BLOCK, BLOCK), 1)
    ).astype(jnp.bfloat16)

    def turn(step, carry):
        for part in range(4):
            at = pl.multiple_of((step * 4 + part) * BLOCK, BLOCK)
            for c, ref in enumerate((q_ref, k_ref, v_ref)):
                tile = ref[:, pl.ds(at, BLOCK)]
                turned[c, pl.ds(at, BLOCK), :] = lax.dot_general(
                    eye, tile, (((1,), (1,)), ((), ())), preferred_element_type=jnp.float32
                ).astype(jnp.bfloat16)
        return carry

    lax.fori_loop(0, D // BLOCK // 4, turn, 0)
    enter(x, p)

    def to_peer(d, slot, part):
        peer = (p + d) % PLANE
        return pltpu.make_async_remote_copy(
            src_ref=turned.at[PARTS[part], head_rows(slot, peer), :],
            dst_ref=group.at[p, slot, PARTS[part]],
            send_sem=send.at[d, slot, part],
            recv_sem=recv.at[p, slot, part],
            device_id=device_of(x, peer),
            device_id_type=MESH,
        )

    def from_peer(j, slot, part):
        return pltpu.make_async_remote_copy(
            src_ref=turned.at[PARTS[part], pl.ds(0, HS), :],
            dst_ref=group.at[j, slot, PARTS[part]],
            send_sem=send.at[0, slot, part],
            recv_sem=recv.at[j, slot, part],
            device_id=device_of(x, (p + 1) % PLANE),
            device_id_type=MESH,
        )

    def near(j, slot):
        return pltpu.make_async_remote_copy(
            src_ref=group.at[j, slot, pl.ds(1, 2)],
            dst_ref=halo.at[8 + j, slot],
            send_sem=halo_send.at[j, slot],
            recv_sem=halo_recv.at[8 + j, slot],
            device_id=device_of((x + 1) % 4, p),
            device_id_type=MESH,
        )

    def far(j):
        return pltpu.make_async_remote_copy(
            src_ref=group.at[j, 1, pl.ds(1, 2)],
            dst_ref=halo.at[j - 24, 1],
            send_sem=far_send.at[j - 24],
            recv_sem=halo_recv.at[j - 24, 1],
            device_id=device_of((x + 2) % 4, p),
            device_id_type=MESH,
        )

    for part in range(2):

        def start_all(d, carry):
            for slot in range(2):
                to_peer(d, slot, part).start()
            return carry

        lax.fori_loop(1, PLANE, start_all, 0)

    own_copies = [
        pltpu.make_async_copy(
            turned.at[:, head_rows(slot, p), :], group.at[p, slot], own.at[slot]
        )
        for slot in range(2)
    ]
    for copy in own_copies:
        copy.start()

    def near_needed(j, slot):
        return (x < 3) & (j >= 33 - most_band(slot, p))

    def far_needed(j):
        return (x < 2) & (j >= 25) & (j >= 65 - most_band(1, p))

    def forward(j, slot):
        @pl.when(near_needed(j, slot))
        def _():
            near(j, slot).start()

        if slot == 1:

            @pl.when(far_needed(j))
            def _():
                far(j).start()

    for slot, copy in enumerate(own_copies):
        copy.wait()
        forward(p, slot)

    def take(d, carry):
        j = (p + PLANE - d) % PLANE
        for slot in range(2):
            from_peer(j, slot, 0).wait_recv()
            forward(j, slot)
        return carry

    lax.fori_loop(1, PLANE, take, 0)

    def finish(d, carry):
        for slot in range(2):
            @pl.when(d > 0)
            def _():
                from_peer((p + d) % PLANE, slot, 1).wait_recv()
                for part in range(2):
                    to_peer(d, slot, part).wait_send()

            @pl.when(near_needed(d, slot))
            def _():
                near(d, slot).wait_send()

            @pl.when((x > 0) & (d >= 33 - most_band(slot, p)))
            def _():
                near(d, slot).wait_recv()

        @pl.when(far_needed(d))
        def _():
            far(d).wait_send()

        @pl.when((x > 1) & (d >= 25) & (d >= 65 - most_band(1, p)))
        def _():
            far(d).wait_recv()

        return carry

    lax.fori_loop(0, PLANE, finish, 0)


def dispatch(query, key, value):
    return pl.pallas_call(
        dispatch_kernel,
        out_shape=(
            jax.ShapeDtypeStruct((PLANE, 2, 3, HS, BLOCK), jnp.bfloat16),
            jax.ShapeDtypeStruct((HALO, 2, 2, HS, BLOCK), jnp.bfloat16),
        ),
        in_specs=[pl.BlockSpec(memory_space=pltpu.VMEM)] * 3,
        out_specs=(pl.BlockSpec(memory_space=pl.ANY), pl.BlockSpec(memory_space=pl.ANY)),
        scratch_shapes=[
            pltpu.VMEM((3, D, BLOCK), jnp.bfloat16),
            pltpu.SemaphoreType.DMA((PLANE, 2, 2)),
            pltpu.SemaphoreType.DMA((PLANE, 2, 2)),
            pltpu.SemaphoreType.DMA((PLANE, 2)),
            pltpu.SemaphoreType.DMA((HALO, 2)),
            pltpu.SemaphoreType.DMA((8,)),
            pltpu.SemaphoreType.DMA((2,)),
        ],
        compiler_params=pltpu.CompilerParams(
            collective_id=0, has_side_effects=True, vmem_limit_bytes=40 << 20
        ),
        name="dispatch",
    )(query, key, value)


PAD = 48
TILE = 4
ROWS = TILE * BLOCK
CHAINS = PLANE // TILE
TAIL = 6


def unit():
    return (
        lax.broadcasted_iota(jnp.int32, (BLOCK, BLOCK), 0)
        == lax.broadcasted_iota(jnp.int32, (BLOCK, BLOCK), 1)
    ).astype(jnp.bfloat16)


def flip(x):
    size = x.shape[1]
    one = (
        lax.broadcasted_iota(jnp.int32, (size, size), 0)
        == lax.broadcasted_iota(jnp.int32, (size, size), 1)
    ).astype(jnp.bfloat16)
    return lax.dot_general(
        one, x, (((1,), (1,)), ((), ())), preferred_element_type=jnp.float32
    ).astype(jnp.bfloat16)


def attend_kernel(
    band_ref, where_ref, slope_ref, group, halo, out, keys, values, queries, acc_ref
):
    x = where_ref[0]
    band = band_ref[pl.program_id(0)]
    factor = HS ** (-0.5)
    scale = factor * LOG2E
    row = lax.broadcasted_iota(jnp.int32, (16, BLOCK), 0)
    token = lax.broadcasted_iota(jnp.int32, (16, BLOCK), 1).astype(jnp.float32)
    ones = jnp.ones((16, BLOCK), jnp.bfloat16)
    nothing = jnp.zeros((HS, BLOCK), jnp.bfloat16)

    def put(index, key_t, value_t, dead):
        block = (index - PAD).astype(jnp.float32)
        extra = jnp.where(
            row < 3, block, jnp.where(row < 6, token, jnp.where(row < 7, dead, 0.0))
        )
        at = pl.multiple_of(index * BLOCK, BLOCK)
        keys[:, pl.ds(at, BLOCK)] = jnp.concatenate([key_t, extra.astype(jnp.bfloat16)], axis=0)
        values[:, pl.ds(at, BLOCK)] = jnp.concatenate([value_t, ones], axis=0)

    def put_pad(index, carry):
        put(index, nothing, nothing, 1.0)
        return carry

    lax.fori_loop(0, PAD - HALO, put_pad, 0)

    def put_halo(step, carry):
        for part in range(4):
            index = step * 4 + part
            live = (index - HALO >= -PLANE * x) & (index - HALO > -band)

            @pl.when(live)
            def _():
                put(index + PAD - HALO, halo[index, 0, 0], halo[index, 0, 1], 0.0)

            @pl.when(jnp.logical_not(live))
            def _():
                put(index + PAD - HALO, nothing, nothing, 1.0)

        return carry

    lax.fori_loop(0, HALO // 4, put_halo, 0)
    slope = slope_ref[0:1, :] * (BLOCK / factor)
    high = slope.astype(jnp.bfloat16).astype(jnp.float32)
    middle = (slope - high).astype(jnp.bfloat16).astype(jnp.float32)
    low = (slope - high - middle).astype(jnp.bfloat16).astype(jnp.float32)
    kind = row % 3
    parts = jnp.where(kind == 0, high, jnp.where(kind == 1, middle, low))
    parts = jnp.where(
        row < 3, parts, jnp.where(row < 6, parts * (1.0 / BLOCK), jnp.where(row < 7, -1e30, 0.0))
    ).astype(jnp.bfloat16)

    def put_group(step, carry):
        for part in range(8):
            index = step * 8 + part
            put(index + PAD, group[index, 0, 1], group[index, 0, 2], 0.0)
            queries[pl.ds(pl.multiple_of(index * BLOCK, BLOCK), BLOCK), :] = flip(
                jnp.concatenate([group[index, 0, 0], parts], axis=0)
            )
        return carry

    lax.fori_loop(0, PLANE // 8, put_group, 0)

    def scores(chain, first, count):
        at = pl.multiple_of((first + PAD) * BLOCK, BLOCK)
        return jnp.dot(
            queries[chain * ROWS : (chain + 1) * ROWS, :],
            keys[:, pl.ds(at, count * BLOCK)],
            preferred_element_type=jnp.float32,
        )

    def mix(first, count, weight):
        at = pl.multiple_of((first + PAD) * BLOCK, BLOCK)
        return lax.dot_general(
            weight.astype(jnp.bfloat16),
            values[:, pl.ds(at, count * BLOCK)],
            (((1,), (1,)), ((), ())),
            preferred_element_type=jnp.float32,
        )

    causal = lax.broadcasted_iota(jnp.int32, (ROWS, ROWS), 1) <= lax.broadcasted_iota(
        jnp.int32, (ROWS, ROWS), 0
    )
    starting = []
    for c in range(CHAINS):
        s = jnp.where(causal, scores(c, c * TILE, TILE), -1e30)
        top = jnp.max(s, axis=1, keepdims=True)
        acc_ref[c] = mix(c * TILE, TILE, jnp.exp2((s - top) * scale))
        starting.append(top)

    def sweep(tops, offset, count, live):
        starts = [c * TILE + offset for c in range(CHAINS)]

        def tile(c):
            s = scores(c, starts[c], count)
            if live is not None:
                s = jnp.where(live, s, -1e30)
            return s, jnp.maximum(tops[c], jnp.max(s, axis=1, keepdims=True))

        after = []
        ready = tile(0)
        for c in range(CHAINS):
            s, new = ready
            if c + 1 < CHAINS:
                ready = tile(c + 1)
            weight = jnp.exp2((s - new) * scale)
            acc_ref[c] = acc_ref[c] * jnp.exp2((tops[c] - new) * scale) + mix(
                starts[c], count, weight
            )
            after.append(new)
        return tuple(after)

    full = (band - TILE) // TILE
    tops = lax.fori_loop(
        0, full, lambda n, tops: sweep(tops, -TILE * n - TILE, TILE, None), tuple(starting)
    )
    key_block = lax.broadcasted_iota(jnp.int32, (ROWS, TAIL * BLOCK), 1) // BLOCK
    query_block = lax.broadcasted_iota(jnp.int32, (ROWS, TAIL * BLOCK), 0) // BLOCK
    offset = -TILE * full - TAIL
    sweep(tops, offset, TAIL, key_block + offset > query_block - band)
    for c in range(CHAINS):
        result = (acc_ref[c, :, 0:HS] / acc_ref[c, :, HS : HS + 1]).astype(jnp.bfloat16)
        for b in range(TILE):
            out[c * TILE + b, 0] = flip(result[b * BLOCK : (b + 1) * BLOCK])


def attend(bands, where, slopes, group, halo):
    return pl.pallas_call(
        attend_kernel,
        out_shape=jax.ShapeDtypeStruct((PLANE, 2, HS, BLOCK), jnp.bfloat16),
        grid_spec=pltpu.PrefetchScalarGridSpec(
            num_scalar_prefetch=2,
            grid=(2,),
            in_specs=[
                pl.BlockSpec((None, 8, BLOCK), lambda i, *_: (i, 0, 0)),
                pl.BlockSpec((PLANE, 1, 3, HS, BLOCK), lambda i, *_: (0, i, 0, 0, 0)),
                pl.BlockSpec((HALO, 1, 2, HS, BLOCK), lambda i, *_: (0, i, 0, 0, 0)),
            ],
            out_specs=pl.BlockSpec((PLANE, 1, HS, BLOCK), lambda i, *_: (0, i, 0, 0)),
            scratch_shapes=[
                pltpu.VMEM((BLOCK, (PAD + PLANE) * BLOCK), jnp.bfloat16),
                pltpu.VMEM((BLOCK, (PAD + PLANE) * BLOCK), jnp.bfloat16),
                pltpu.VMEM((PLANE * BLOCK, BLOCK), jnp.bfloat16),
                pltpu.VMEM((CHAINS, ROWS, BLOCK), jnp.float32),
            ],
        ),
        compiler_params=pltpu.CompilerParams(
            dimension_semantics=("arbitrary",), vmem_limit_bytes=56 << 20
        ),
        name="attend",
    )(bands, where, slopes, group, halo)


def combine_kernel(mixed, out, back, send, recv, own):
    x, p = coords()
    enter(x, p)

    def to_peer(d, slot):
        peer = (p + d) % PLANE
        return pltpu.make_async_remote_copy(
            src_ref=mixed.at[peer, slot],
            dst_ref=back.at[head_rows(slot, p), :],
            send_sem=send.at[d, slot],
            recv_sem=recv.at[p, slot],
            device_id=device_of(x, peer),
            device_id_type=MESH,
        )

    def from_peer(j, slot):
        return pltpu.make_async_remote_copy(
            src_ref=mixed.at[0, slot],
            dst_ref=back.at[head_rows(slot, j), :],
            send_sem=send.at[0, slot],
            recv_sem=recv.at[j, slot],
            device_id=device_of(x, (p + 1) % PLANE),
            device_id_type=MESH,
        )

    def start_all(d, carry):
        for slot in range(2):
            to_peer(d, slot).start()
        return carry

    lax.fori_loop(1, PLANE, start_all, 0)
    for slot in range(2):
        copy = pltpu.make_async_copy(
            mixed.at[p, slot], back.at[head_rows(slot, p), :], own.at[slot]
        )
        copy.start()
        copy.wait()

    def finish(d, carry):
        j = (p + PLANE - d) % PLANE
        for slot in range(2):
            from_peer(j, slot).wait_recv()
            to_peer(d, slot).wait_send()
        return carry

    lax.fori_loop(1, PLANE, finish, 0)
    eye = (
        lax.broadcasted_iota(jnp.int32, (BLOCK, BLOCK), 0)
        == lax.broadcasted_iota(jnp.int32, (BLOCK, BLOCK), 1)
    ).astype(jnp.bfloat16)

    def turn(step, carry):
        for part in range(4):
            at = pl.multiple_of((step * 4 + part) * BLOCK, BLOCK)
            out[:, pl.ds(at, BLOCK)] = lax.dot_general(
                eye, back[pl.ds(at, BLOCK), :], (((1,), (1,)), ((), ())),
                preferred_element_type=jnp.float32,
            ).astype(jnp.bfloat16)
        return carry

    lax.fori_loop(0, D // BLOCK // 4, turn, 0)


def combine(mixed):
    return pl.pallas_call(
        combine_kernel,
        out_shape=jax.ShapeDtypeStruct((BLOCK, D), jnp.bfloat16),
        in_specs=[pl.BlockSpec(memory_space=pltpu.VMEM)],
        out_specs=pl.BlockSpec(memory_space=pltpu.VMEM),
        scratch_shapes=[
            pltpu.VMEM((D, BLOCK), jnp.bfloat16),
            pltpu.SemaphoreType.DMA((PLANE, 2)),
            pltpu.SemaphoreType.DMA((PLANE, 2)),
            pltpu.SemaphoreType.DMA((2,)),
        ],
        compiler_params=pltpu.CompilerParams(
            collective_id=1, has_side_effects=True, vmem_limit_bytes=40 << 20
        ),
        name="combine",
    )(mixed)


def on_device(query, key, value, exponent):
    x, p = coords()
    heads = jnp.stack([p, HEADS - 1 - p])
    local = jnp.take(exponent, heads)
    bands = MIN_BAND + (local - 1) * (MAX_BAND - MIN_BAND) // (HEADS - 1)
    slopes = jnp.exp2(-12.0 * local.astype(jnp.float32) / HEADS)
    slopes = jnp.broadcast_to(slopes[:, None, None], (2, 8, BLOCK))
    group, halo = dispatch(query, key, value)
    mixed = attend(bands, x[None], slopes, group, halo)
    return combine(mixed)


def solution(mesh):
    return jax.shard_map(
        on_device,
        mesh=mesh,
        in_specs=(
            P(("seq", "head"), None),
            P(("seq", "head"), None),
            P(("seq", "head"), None),
            P(),
        ),
        out_specs=P(("seq", "head"), None),
        check_vma=False,
    )
```

```python
import jax
import jax.numpy as jnp
from jax import lax
from jax.experimental import pallas as pl
from jax.experimental.pallas import tpu as pltpu
from jax.sharding import PartitionSpec as P

BLOCK = 128
MIN_BAND = 16
MAX_BAND = 40
HEADS = 64
HS = 112
D = HEADS * HS
HALF = D // 2
PLANE = 32
PAD = 48
TILE = 4
ROWS = TILE * BLOCK
CHAINS = PLANE // TILE
MESH = pl.DeviceIdType.MESH
LOG2E = 1.4426950408889634
FACTOR = HS ** (-0.5)
SCALE = FACTOR * LOG2E
PARTS = (pl.ds(1, 2), pl.ds(0, 1))


def coords():
    seq = lax.axis_index("seq")
    head = lax.axis_index("head")
    x = seq // 4
    p = (seq % 4) * 8 + head
    return x, p


def device_of(x, p):
    return (x * 4 + p // 8, p % 8)


def past_six(p):
    return (p - 6) * ((p + 26) // 32)


def most_band(slot, p):
    low = (p + 6) * 24 // 63
    high = (63 - past_six(p)) * 24 // 63
    return MIN_BAND + low + slot * (high - low)


def least_band(slot, p):
    low = past_six(p) * 24 // 63
    high = (57 - p) * 24 // 63
    return MIN_BAND + low + slot * (high - low)


def head_rows(slot, p):
    head = p + slot * (HEADS - 1 - 2 * p)
    return pl.ds(pl.multiple_of(head * HS, 16), HS)


def lanes(block):
    return pl.ds(pl.multiple_of(block * BLOCK, BLOCK), BLOCK)


def flip(x):
    size = x.shape[1]
    one = (
        lax.broadcasted_iota(jnp.int32, (size, size), 0)
        == lax.broadcasted_iota(jnp.int32, (size, size), 1)
    ).astype(jnp.bfloat16)
    return lax.dot_general(
        one, x, (((1,), (1,)), ((), ())), preferred_element_type=jnp.float32
    ).astype(jnp.bfloat16)


def enter(x, p):
    barrier = pltpu.get_barrier_semaphore()

    def greet(d, carry):
        pl.semaphore_signal(
            barrier, inc=1, device_id=device_of(x, (p + d) % PLANE), device_id_type=MESH
        )
        return carry

    lax.fori_loop(1, PLANE, greet, 0)
    for d in range(1, 4):
        pl.semaphore_signal(
            barrier, inc=1, device_id=device_of((x + d) % 4, p), device_id_type=MESH
        )
    pl.semaphore_wait(barrier, PLANE - 1 + 3)


def layer_kernel(
    band_ref,
    slope_ref,
    q_hbm,
    k_hbm,
    v_hbm,
    out_hbm,
    staged,
    turned,
    kv,
    arrived,
    queries,
    acc_ref,
    mixed,
    back,
    result_ref,
    load,
    send,
    recv,
    own,
    halo_send,
    halo_recv,
    far_send,
    back_send,
    back_recv,
    store,
):
    x, p = coords()

    def load_copy(c, half):
        columns = pl.ds(half * HALF, HALF)
        return pltpu.make_async_copy(
            (q_hbm, k_hbm, v_hbm)[c].at[:, columns], staged.at[c, :, columns], load.at[c, half]
        )

    for half in (1, 0):
        for c in (1, 2, 0):
            load_copy(c, half).start()

    row = lax.broadcasted_iota(jnp.int32, (16, BLOCK), 0)
    token = lax.broadcasted_iota(jnp.int32, (16, BLOCK), 1).astype(jnp.float32)

    for slot in range(2):

        def prepare(index, carry):
            block = index - PAD
            absent = (block < -PLANE * x) | (block <= -most_band(slot, p))
            extra = jnp.where(
                row < 3,
                block.astype(jnp.float32),
                jnp.where(row < 6, token, jnp.where(row < 7, jnp.where(absent, 1.0, 0.0), 0.0)),
            )
            kv[slot, 0, HS:BLOCK, lanes(index)] = extra.astype(jnp.bfloat16)
            kv[slot, 1, HS:BLOCK, lanes(index)] = jnp.ones((16, BLOCK), jnp.bfloat16)

            @pl.when(absent)
            def _():
                for c in range(2):
                    kv[slot, c, 0:HS, lanes(index)] = jnp.zeros((HS, BLOCK), jnp.bfloat16)

            return carry

        lax.fori_loop(0, PAD + PLANE, prepare, 0)

    def turn_half(half):
        def turn(step, carry):
            for part in range(7):
                at = lanes(half * 28 + step * 7 + part)
                for c in range(3):
                    turned[c, at, :] = flip(staged[c, :, at])
            return carry

        for c in range(3):
            load_copy(c, half).wait()
        lax.fori_loop(0, 4, turn, 0)

    def message(j, slot, part, place, peer, sem):
        source = turned.at[PARTS[part], head_rows(slot, place), :]
        if part == 0:
            target = kv.at[slot, :, pl.ds(0, HS), lanes(PAD + j)]
        else:
            target = arrived.at[pl.ds(slot, 1), j]
        return pltpu.make_async_remote_copy(
            src_ref=source,
            dst_ref=target,
            send_sem=send.at[sem, slot, part],
            recv_sem=recv.at[j, slot, part],
            device_id=device_of(x, peer),
            device_id_type=MESH,
        )

    def to_peer(d, slot, part):
        peer = (p + d) % PLANE
        return message(p, slot, part, peer, peer, d)

    def from_peer(j, slot, part):
        return message(j, slot, part, 0, (p + 1) % PLANE, 0)

    def own_copy(slot, part):
        if part == 0:
            target = kv.at[slot, :, pl.ds(0, HS), lanes(PAD + p)]
        else:
            target = arrived.at[pl.ds(slot, 1), p]
        return pltpu.make_async_copy(
            turned.at[PARTS[part], head_rows(slot, p), :], target, own.at[slot, part]
        )

    def near(j, slot):
        return pltpu.make_async_remote_copy(
            src_ref=kv.at[slot, :, pl.ds(0, HS), lanes(PAD + j)],
            dst_ref=kv.at[slot, :, pl.ds(0, HS), lanes(PAD - PLANE + j)],
            send_sem=halo_send.at[j, slot],
            recv_sem=halo_recv.at[8 + j, slot],
            device_id=device_of((x + 1) % 4, p),
            device_id_type=MESH,
        )

    def far(j):
        return pltpu.make_async_remote_copy(
            src_ref=kv.at[1, :, pl.ds(0, HS), lanes(PAD + j)],
            dst_ref=kv.at[1, :, pl.ds(0, HS), lanes(PAD - 2 * PLANE + j)],
            send_sem=far_send.at[j - 24],
            recv_sem=halo_recv.at[j - 24, 1],
            device_id=device_of((x + 2) % 4, p),
            device_id_type=MESH,
        )

    def near_needed(j, slot):
        return j >= 33 - most_band(slot, p)

    def far_needed(j):
        return (j >= 25) & (j >= 65 - most_band(1, p))

    def forward(j, slot):
        @pl.when((x < 3) & near_needed(j, slot))
        def _():
            near(j, slot).start()

        if slot == 1:

            @pl.when((x < 2) & far_needed(j))
            def _():
                far(j).start()

    def start_slot(slot):
        for part in range(2):

            def start(d, carry):
                to_peer(d, slot, part).start()
                return carry

            lax.fori_loop(1, PLANE, start, 0)
            own_copy(slot, part).start()

    turn_half(1)
    enter(x, p)
    start_slot(1)
    turn_half(0)
    start_slot(0)

    def take(d, slot):
        j = (p + PLANE - d) % PLANE
        from_peer(j, slot, 0).wait_recv()
        forward(j, slot)

    for slot in (1, 0):
        own_copy(slot, 0).wait()
        forward(p, slot)

    def take_heavy(d, carry):
        take(d, 1)
        return carry

    lax.fori_loop(1, PLANE, take_heavy, 0)

    causal = lax.broadcasted_iota(jnp.int32, (ROWS, ROWS), 1) <= lax.broadcasted_iota(
        jnp.int32, (ROWS, ROWS), 0
    )

    def send_back(block, slot):
        return pltpu.make_async_remote_copy(
            src_ref=mixed.at[slot, block],
            dst_ref=back.at[head_rows(slot, p), :],
            send_sem=back_send.at[block, slot],
            recv_sem=back_recv.at[p, slot],
            device_id=device_of(x, block),
            device_id_type=MESH,
        )

    def keep_back(slot):
        return pltpu.make_async_copy(
            mixed.at[slot, p], back.at[head_rows(slot, p), :], back_recv.at[p, slot]
        )

    def got_back(j, slot):
        return pltpu.make_async_remote_copy(
            src_ref=mixed.at[slot, 0],
            dst_ref=back.at[head_rows(slot, j), :],
            send_sem=back_send.at[0, slot],
            recv_sem=back_recv.at[j, slot],
            device_id=device_of(x, (p + 1) % PLANE),
            device_id_type=MESH,
        )

    def attend(slot):
        band = band_ref[slot]

        own_copy(slot, 1).wait()

        def take_query(d, carry):
            from_peer((p + PLANE - d) % PLANE, slot, 1).wait_recv()
            return carry

        lax.fori_loop(1, PLANE, take_query, 0)
        slope = slope_ref[slot, 0:1, :] * (BLOCK / FACTOR)
        high = slope.astype(jnp.bfloat16).astype(jnp.float32)
        middle = (slope - high).astype(jnp.bfloat16).astype(jnp.float32)
        low = (slope - high - middle).astype(jnp.bfloat16).astype(jnp.float32)
        kind = row % 3
        parts = jnp.where(kind == 0, high, jnp.where(kind == 1, middle, low))
        parts = jnp.where(
            row < 3,
            parts,
            jnp.where(row < 6, parts * (1.0 / BLOCK), jnp.where(row < 7, -1e30, 0.0)),
        ).astype(jnp.bfloat16)

        def put_queries(step, carry):
            for part in range(8):
                index = step * 8 + part
                queries[lanes(index), :] = flip(
                    jnp.concatenate([arrived[slot, index], parts], axis=0)
                )
            return carry

        lax.fori_loop(0, PLANE // 8, put_queries, 0)

        def take_halo(j, carry):
            @pl.when((x > 0) & near_needed(j, slot))
            def _():
                near(j, slot).wait_recv()

            if slot == 1:

                @pl.when((x > 1) & far_needed(j))
                def _():
                    far(j).wait_recv()

            return carry

        def scores(chain, first):
            at = pl.multiple_of((first + PAD) * BLOCK, BLOCK)
            return jnp.dot(
                queries[chain * ROWS : (chain + 1) * ROWS, :],
                kv[slot, 0, :, pl.ds(at, ROWS)],
                preferred_element_type=jnp.float32,
            )

        def mix(first, weight):
            at = pl.multiple_of((first + PAD) * BLOCK, BLOCK)
            return lax.dot_general(
                weight.astype(jnp.bfloat16),
                kv[slot, 1, :, pl.ds(at, ROWS)],
                (((1,), (1,)), ((), ())),
                preferred_element_type=jnp.float32,
            )

        def sweep(tops, offset, kind):
            starts = [c * TILE + offset for c in range(CHAINS)]

            def tile(c):
                s = scores(c, starts[c])
                if kind == "first":
                    s = jnp.where(causal, s, -1e30)
                    return s, jnp.max(s, axis=1, keepdims=True)
                if kind == "edge":
                    rows = []
                    for r in range(TILE):
                        columns = []
                        for k in range(TILE):
                            far_off = jnp.where(offset + (k - r) > -band, 0.0, -1e30)
                            columns.append(
                                s[r * BLOCK : (r + 1) * BLOCK, k * BLOCK : (k + 1) * BLOCK]
                                + far_off
                            )
                        rows.append(jnp.concatenate(columns, axis=1))
                    s = jnp.concatenate(rows, axis=0)
                return s, jnp.maximum(tops[c], jnp.max(s, axis=1, keepdims=True))

            after = []
            ready = tile(0)
            for c in range(CHAINS):
                s, new = ready
                if c + 1 < CHAINS:
                    ready = tile(c + 1)
                fresh = mix(starts[c], jnp.exp2((s - new) * SCALE))
                if kind == "first":
                    acc_ref[c] = fresh
                else:
                    acc_ref[c] = acc_ref[c] * jnp.exp2((tops[c] - new) * SCALE) + fresh
                after.append(new)
            return tuple(after)

        tops = sweep(None, 0, "first")
        lax.fori_loop(0, PLANE, take_halo, 0)
        full = (least_band(slot, p) - TILE) // TILE
        total = (most_band(slot, p) + 2) // TILE

        def inner(n, tops):
            if slot == 1:
                for part in range(7):
                    d = 1 + n * 7 + part

                    @pl.when(d < PLANE)
                    def _():
                        take(d, 0)

            return sweep(tops, -TILE * (n + 1), "inner")

        tops = lax.fori_loop(0, full, inner, tops)
        lax.fori_loop(
            full, total, lambda n, tops: sweep(tops, -TILE * (n + 1), "edge"), tops
        )
        for c in range(CHAINS):
            result = (acc_ref[c, :, 0:HS] / acc_ref[c, :, HS : HS + 1]).astype(jnp.bfloat16)
            for b in range(TILE):
                block = c * TILE + b
                mixed[slot, block] = flip(result[b * BLOCK : (b + 1) * BLOCK])

        def give(d, carry):
            send_back((p + d) % PLANE, slot).start()
            return carry

        lax.fori_loop(1, PLANE, give, 0)
        keep_back(slot).start()

    attend(1)
    attend(0)

    def unturn_half(half):
        def arrive(d, carry):
            got_back((p + PLANE - d) % PLANE, half).wait_recv()
            return carry

        keep_back(half).wait()
        lax.fori_loop(1, PLANE, arrive, 0)

        def unturn(step, carry):
            for part in range(7):
                at = lanes(half * 28 + step * 7 + part)
                result_ref[:, at] = flip(back[at, :])
            return carry

        lax.fori_loop(0, 4, unturn, 0)
        columns = pl.ds(half * HALF, HALF)
        copy = pltpu.make_async_copy(
            result_ref.at[:, columns], out_hbm.at[:, columns], store.at[half]
        )
        copy.start()
        return copy

    stores = [unturn_half(1), unturn_half(0)]

    def finish(d, carry):
        for slot in range(2):

            @pl.when(d > 0)
            def _():
                for part in range(2):
                    to_peer(d, slot, part).wait_send()
                send_back((p + d) % PLANE, slot).wait_send()

            @pl.when((x < 3) & near_needed(d, slot))
            def _():
                near(d, slot).wait_send()

        @pl.when((x < 2) & far_needed(d))
        def _():
            far(d).wait_send()

        return carry

    lax.fori_loop(0, PLANE, finish, 0)
    for copy in stores:
        copy.wait()


def layer(bands, slopes, query, key, value):
    anywhere = pl.BlockSpec(memory_space=pl.ANY)
    return pl.pallas_call(
        layer_kernel,
        out_shape=jax.ShapeDtypeStruct((BLOCK, D), jnp.bfloat16),
        in_specs=[
            pl.BlockSpec(memory_space=pltpu.SMEM),
            pl.BlockSpec(memory_space=pltpu.VMEM),
            anywhere,
            anywhere,
            anywhere,
        ],
        out_specs=anywhere,
        scratch_shapes=[
            pltpu.VMEM((3, BLOCK, D), jnp.bfloat16),
            pltpu.VMEM((3, D, BLOCK), jnp.bfloat16),
            pltpu.VMEM((2, 2, BLOCK, (PAD + PLANE) * BLOCK), jnp.bfloat16),
            pltpu.VMEM((2, PLANE, HS, BLOCK), jnp.bfloat16),
            pltpu.VMEM((PLANE * BLOCK, BLOCK), jnp.bfloat16),
            pltpu.VMEM((CHAINS, ROWS, BLOCK), jnp.float32),
            pltpu.VMEM((2, PLANE, HS, BLOCK), jnp.bfloat16),
            pltpu.VMEM((D, BLOCK), jnp.bfloat16),
            pltpu.VMEM((BLOCK, D), jnp.bfloat16),
            pltpu.SemaphoreType.DMA((3, 2)),
            pltpu.SemaphoreType.DMA((PLANE, 2, 2)),
            pltpu.SemaphoreType.DMA((PLANE, 2, 2)),
            pltpu.SemaphoreType.DMA((2, 2)),
            pltpu.SemaphoreType.DMA((PLANE, 2)),
            pltpu.SemaphoreType.DMA((8 + PLANE, 2)),
            pltpu.SemaphoreType.DMA((8,)),
            pltpu.SemaphoreType.DMA((PLANE, 2)),
            pltpu.SemaphoreType.DMA((PLANE, 2)),
            pltpu.SemaphoreType.DMA((2,)),
        ],
        compiler_params=pltpu.CompilerParams(
            collective_id=0, has_side_effects=True, vmem_limit_bytes=60 << 20
        ),
        name="layer",
    )(bands, slopes, query, key, value)


def on_device(query, key, value, exponent):
    x, p = coords()
    heads = jnp.stack([p, HEADS - 1 - p])
    local = jnp.take(exponent, heads)
    bands = MIN_BAND + (local - 1) * (MAX_BAND - MIN_BAND) // (HEADS - 1)
    slopes = jnp.exp2(-12.0 * local.astype(jnp.float32) / HEADS)
    slopes = jnp.broadcast_to(slopes[:, None, None], (2, 8, BLOCK))
    return layer(bands, slopes, query, key, value)


def solution(mesh):
    return jax.shard_map(
        on_device,
        mesh=mesh,
        in_specs=(
            P(("seq", "head"), None),
            P(("seq", "head"), None),
            P(("seq", "head"), None),
            P(),
        ),
        out_specs=P(("seq", "head"), None),
        check_vma=False,
    )
```

```python
import jax
import jax.numpy as jnp
from jax import lax
from jax.experimental import pallas as pl
from jax.experimental.pallas import tpu as pltpu
from jax.sharding import PartitionSpec as P

BLOCK = 128
MIN_BAND = 16
MAX_BAND = 40
HEADS = 64
HS = 112
D = HEADS * HS
HALF = D // 2
PLANE = 32
PAD = 48
TILE = 4
ROWS = TILE * BLOCK
STRIDE = 11
CHAINS = PLANE // TILE
MESH = pl.DeviceIdType.MESH
LOG2E = 1.4426950408889634
FACTOR = HS ** (-0.5)
SCALE = FACTOR * LOG2E
PARTS = (pl.ds(1, 2), pl.ds(0, 1))


def coords():
    seq = lax.axis_index("seq")
    head = lax.axis_index("head")
    x = seq // 4
    p = (seq % 4) * 8 + head
    return x, p


def device_of(x, p):
    return (x * 4 + p // 8, p % 8)


def past_six(p):
    return (p - 6) * ((p + 26) // 32)


def most_band(slot, p):
    low = (p + 6) * 24 // 63
    high = (63 - past_six(p)) * 24 // 63
    return MIN_BAND + low + slot * (high - low)


def least_band(slot, p):
    low = past_six(p) * 24 // 63
    high = (57 - p) * 24 // 63
    return MIN_BAND + low + slot * (high - low)


def head_rows(slot, p):
    head = p + slot * (HEADS - 1 - 2 * p)
    return pl.ds(pl.multiple_of(head * HS, 16), HS)


def lanes(block):
    return pl.ds(pl.multiple_of(block * BLOCK, BLOCK), BLOCK)


def flip(x):
    size = x.shape[1]
    one = (
        lax.broadcasted_iota(jnp.int32, (size, size), 0)
        == lax.broadcasted_iota(jnp.int32, (size, size), 1)
    ).astype(jnp.bfloat16)
    return lax.dot_general(
        one, x, (((1,), (1,)), ((), ())), preferred_element_type=jnp.float32
    ).astype(jnp.bfloat16)


def greet_all(x, p):
    barrier = pltpu.get_barrier_semaphore()

    def greet(d, carry):
        pl.semaphore_signal(
            barrier, inc=1, device_id=device_of(x, (p + d) % PLANE), device_id_type=MESH
        )
        return carry

    lax.fori_loop(1, PLANE, greet, 0)
    for d in range(1, 4):
        pl.semaphore_signal(
            barrier, inc=1, device_id=device_of((x + d) % 4, p), device_id_type=MESH
        )
    return barrier


def layer_kernel(
    exponent_ref,
    q_hbm,
    k_hbm,
    v_hbm,
    out_hbm,
    staged,
    turned,
    kv,
    arrived,
    queries,
    acc_ref,
    mixed,
    back,
    result_ref,
    load,
    send,
    recv,
    own,
    halo_send,
    halo_recv,
    far_send,
    back_send,
    back_recv,
    store,
):
    x, p = coords()

    def load_copy(c, half):
        columns = pl.ds(half * HALF, HALF)
        return pltpu.make_async_copy(
            (q_hbm, k_hbm, v_hbm)[c].at[:, columns], staged.at[c, :, columns], load.at[c, half]
        )

    for half in (1, 0):
        for c in (1, 2, 0):
            load_copy(c, half).start()

    barrier = greet_all(x, p)
    row = lax.broadcasted_iota(jnp.int32, (16, BLOCK), 0)
    token = lax.broadcasted_iota(jnp.int32, (16, BLOCK), 1).astype(jnp.float32)

    def absent(index, slot):
        block = index - PAD
        return (block < -PLANE * x) | (block <= -most_band(slot, p))

    def prepare():
        ones = jnp.ones((16, BLOCK), jnp.bfloat16)
        zeros = jnp.zeros((HS, BLOCK), jnp.bfloat16)
        for slot in range(2):

            def extras(step, carry):
                for part in range(8):
                    index = step * 8 + part
                    block = (index - PAD).astype(jnp.float32)
                    dead = jnp.where(absent(index, slot), 1.0, 0.0)
                    extra = jnp.where(
                        row < 3, block, jnp.where(row < 6, token, jnp.where(row < 7, dead, 0.0))
                    )
                    kv[slot, 0, HS:BLOCK, lanes(index)] = extra.astype(jnp.bfloat16)
                    kv[slot, 1, HS:BLOCK, lanes(index)] = ones
                return carry

            lax.fori_loop(0, (PAD + PLANE) // 8, extras, 0)

            def clear(index, carry):
                @pl.when(absent(index, slot))
                def _():
                    for c in range(2):
                        kv[slot, c, 0:HS, lanes(index)] = zeros

                return carry

            lax.fori_loop(0, PAD, clear, 0)

    def turn_half(half, tensors):
        def turn(step, carry):
            for part in range(7):
                at = lanes(half * 28 + step * 7 + part)
                for c in tensors:
                    turned[c, at, :] = flip(staged[c, :, at])
            return carry

        for c in tensors:
            load_copy(c, half).wait()
        lax.fori_loop(0, 4, turn, 0)

    def message(j, slot, part, place, peer, sem):
        source = turned.at[PARTS[part], head_rows(slot, place), :]
        if part == 0:
            target = kv.at[slot, :, pl.ds(0, HS), lanes(PAD + j)]
        else:
            target = arrived.at[pl.ds(slot, 1), j]
        return pltpu.make_async_remote_copy(
            src_ref=source,
            dst_ref=target,
            send_sem=send.at[sem, slot, part],
            recv_sem=recv.at[j, slot, part],
            device_id=device_of(x, peer),
            device_id_type=MESH,
        )

    def to_peer(d, slot, part):
        peer = (p + STRIDE * d) % PLANE
        return message(p, slot, part, peer, peer, d)

    def from_peer(j, slot, part):
        return message(j, slot, part, 0, (p + 1) % PLANE, 0)

    def own_copy(slot, part):
        if part == 0:
            target = kv.at[slot, :, pl.ds(0, HS), lanes(PAD + p)]
        else:
            target = arrived.at[pl.ds(slot, 1), p]
        return pltpu.make_async_copy(
            turned.at[PARTS[part], head_rows(slot, p), :], target, own.at[slot, part]
        )

    def near(j, slot):
        return pltpu.make_async_remote_copy(
            src_ref=kv.at[slot, :, pl.ds(0, HS), lanes(PAD + j)],
            dst_ref=kv.at[slot, :, pl.ds(0, HS), lanes(PAD - PLANE + j)],
            send_sem=halo_send.at[j, slot],
            recv_sem=halo_recv.at[8 + j, slot],
            device_id=device_of((x + 1) % 4, p),
            device_id_type=MESH,
        )

    def far(j):
        return pltpu.make_async_remote_copy(
            src_ref=kv.at[1, :, pl.ds(0, HS), lanes(PAD + j)],
            dst_ref=kv.at[1, :, pl.ds(0, HS), lanes(PAD - 2 * PLANE + j)],
            send_sem=far_send.at[j - 24],
            recv_sem=halo_recv.at[j - 24, 1],
            device_id=device_of((x + 2) % 4, p),
            device_id_type=MESH,
        )

    def near_needed(j, slot):
        return j >= 33 - most_band(slot, p)

    def far_needed(j):
        return (j >= 25) & (j >= 65 - most_band(1, p))

    def forward(j, slot):
        @pl.when((x < 3) & near_needed(j, slot))
        def _():
            near(j, slot).start()

        if slot == 1:

            @pl.when((x < 2) & far_needed(j))
            def _():
                far(j).start()

    def start_part(slot, part):
        def start(d, carry):
            to_peer(d, slot, part).start()
            return carry

        lax.fori_loop(1, PLANE, start, 0)
        own_copy(slot, part).start()

    turn_half(1, (1, 2))
    pl.semaphore_wait(barrier, PLANE - 1 + 3)
    start_part(1, 0)
    turn_half(1, (0,))
    start_part(1, 1)
    turn_half(0, (1, 2))
    start_part(0, 0)
    turn_half(0, (0,))
    start_part(0, 1)
    prepare()

    def take(d, slot):
        j = (p + STRIDE * (PLANE - d)) % PLANE
        from_peer(j, slot, 0).wait_recv()
        forward(j, slot)

    for slot in (1, 0):
        own_copy(slot, 0).wait()
        forward(p, slot)

    def take_heavy(d, carry):
        take(d, 1)
        return carry

    lax.fori_loop(1, PLANE, take_heavy, 0)

    causal = lax.broadcasted_iota(jnp.int32, (ROWS, ROWS), 1) <= lax.broadcasted_iota(
        jnp.int32, (ROWS, ROWS), 0
    )

    def send_back(block, slot):
        return pltpu.make_async_remote_copy(
            src_ref=mixed.at[slot, block],
            dst_ref=back.at[head_rows(slot, p), :],
            send_sem=back_send.at[block, slot],
            recv_sem=back_recv.at[p, slot],
            device_id=device_of(x, block),
            device_id_type=MESH,
        )

    def keep_back(slot):
        return pltpu.make_async_copy(
            mixed.at[slot, p], back.at[head_rows(slot, p), :], back_recv.at[p, slot]
        )

    def got_back(j, slot):
        return pltpu.make_async_remote_copy(
            src_ref=mixed.at[slot, 0],
            dst_ref=back.at[head_rows(slot, j), :],
            send_sem=back_send.at[0, slot],
            recv_sem=back_recv.at[j, slot],
            device_id=device_of(x, (p + 1) % PLANE),
            device_id_type=MESH,
        )

    def attend(slot):
        exponent = exponent_ref[p + slot * (HEADS - 1 - 2 * p)]
        band = MIN_BAND + (exponent - 1) * (MAX_BAND - MIN_BAND) // (HEADS - 1)
        power = jnp.full((1, BLOCK), exponent.astype(jnp.float32)) * (-12.0 / HEADS)

        own_copy(slot, 1).wait()

        def take_query(d, carry):
            from_peer((p + STRIDE * (PLANE - d)) % PLANE, slot, 1).wait_recv()
            return carry

        lax.fori_loop(1, PLANE, take_query, 0)
        slope = jnp.exp2(power) * (BLOCK / FACTOR)
        high = slope.astype(jnp.bfloat16).astype(jnp.float32)
        middle = (slope - high).astype(jnp.bfloat16).astype(jnp.float32)
        low = (slope - high - middle).astype(jnp.bfloat16).astype(jnp.float32)
        kind = row % 3
        parts = jnp.where(kind == 0, high, jnp.where(kind == 1, middle, low))
        parts = jnp.where(
            row < 3,
            parts,
            jnp.where(row < 6, parts * (1.0 / BLOCK), jnp.where(row < 7, -1e30, 0.0)),
        ).astype(jnp.bfloat16)

        def put_queries(step, carry):
            for part in range(8):
                index = step * 8 + part
                queries[lanes(index), :] = flip(
                    jnp.concatenate([arrived[slot, index], parts], axis=0)
                )
            return carry

        lax.fori_loop(0, PLANE // 8, put_queries, 0)

        def take_halo(j, carry):
            @pl.when((x > 0) & near_needed(j, slot))
            def _():
                near(j, slot).wait_recv()

            if slot == 1:

                @pl.when((x > 1) & far_needed(j))
                def _():
                    far(j).wait_recv()

            return carry

        def scores(chain, first):
            at = pl.multiple_of((first + PAD) * BLOCK, BLOCK)
            return jnp.dot(
                queries[chain * ROWS : (chain + 1) * ROWS, :],
                kv[slot, 0, :, pl.ds(at, ROWS)],
                preferred_element_type=jnp.float32,
            )

        def mix(first, weight):
            at = pl.multiple_of((first + PAD) * BLOCK, BLOCK)
            return lax.dot_general(
                weight.astype(jnp.bfloat16),
                kv[slot, 1, :, pl.ds(at, ROWS)],
                (((1,), (1,)), ((), ())),
                preferred_element_type=jnp.float32,
            )

        def sweep(tops, offset, kind):
            starts = [c * TILE + offset for c in range(CHAINS)]

            def tile(c):
                s = scores(c, starts[c])
                if kind == "first":
                    s = jnp.where(causal, s, -1e30)
                    return s, jnp.max(s, axis=1, keepdims=True)
                if kind == "edge":
                    rows = []
                    for r in range(TILE):
                        columns = []
                        for k in range(TILE):
                            far_off = jnp.where(offset + (k - r) > -band, 0.0, -1e30)
                            columns.append(
                                s[r * BLOCK : (r + 1) * BLOCK, k * BLOCK : (k + 1) * BLOCK]
                                + far_off
                            )
                        rows.append(jnp.concatenate(columns, axis=1))
                    s = jnp.concatenate(rows, axis=0)
                return s, jnp.maximum(tops[c], jnp.max(s, axis=1, keepdims=True))

            after = []
            ready = tile(0)
            for c in range(CHAINS):
                s, new = ready
                if c + 1 < CHAINS:
                    ready = tile(c + 1)
                fresh = mix(starts[c], jnp.exp2((s - new) * SCALE))
                if kind == "first":
                    acc_ref[c] = fresh
                else:
                    acc_ref[c] = acc_ref[c] * jnp.exp2((tops[c] - new) * SCALE) + fresh
                after.append(new)
            return tuple(after)

        tops = sweep(None, 0, "first")
        lax.fori_loop(0, PLANE, take_halo, 0)
        full = (least_band(slot, p) - TILE) // TILE
        total = (most_band(slot, p) + 2) // TILE

        def inner(n, tops):
            if slot == 1:
                for part in range(7):
                    d = 1 + n * 7 + part

                    @pl.when(d < PLANE)
                    def _():
                        take(d, 0)

            return sweep(tops, -TILE * (n + 1), "inner")

        tops = lax.fori_loop(0, full, inner, tops)
        lax.fori_loop(
            full, total, lambda n, tops: sweep(tops, -TILE * (n + 1), "edge"), tops
        )
        for c in range(CHAINS):
            result = (acc_ref[c, :, 0:HS] / acc_ref[c, :, HS : HS + 1]).astype(jnp.bfloat16)
            for b in range(TILE):
                block = c * TILE + b
                mixed[slot, block] = flip(result[b * BLOCK : (b + 1) * BLOCK])

        def give(d, carry):
            send_back((p + STRIDE * d) % PLANE, slot).start()
            return carry

        lax.fori_loop(1, PLANE, give, 0)
        keep_back(slot).start()

    attend(1)
    attend(0)

    def unturn_half(half):
        def arrive(d, carry):
            got_back((p + STRIDE * (PLANE - d)) % PLANE, half).wait_recv()
            return carry

        keep_back(half).wait()
        lax.fori_loop(1, PLANE, arrive, 0)

        def unturn(step, carry):
            for part in range(7):
                at = lanes(half * 28 + step * 7 + part)
                result_ref[:, at] = flip(back[at, :])
            return carry

        lax.fori_loop(0, 4, unturn, 0)
        columns = pl.ds(half * HALF, HALF)
        copy = pltpu.make_async_copy(
            result_ref.at[:, columns], out_hbm.at[:, columns], store.at[half]
        )
        copy.start()
        return copy

    stores = [unturn_half(1)]

    def finish(d, carry):
        for slot in range(2):

            @pl.when(d > 0)
            def _():
                for part in range(2):
                    to_peer(d, slot, part).wait_send()

            @pl.when((x < 3) & near_needed(d, slot))
            def _():
                near(d, slot).wait_send()

        @pl.when((x < 2) & far_needed(d))
        def _():
            far(d).wait_send()

        return carry

    lax.fori_loop(0, PLANE, finish, 0)
    stores.append(unturn_half(0))

    def finish_back(d, carry):
        for slot in range(2):
            send_back((p + d) % PLANE, slot).wait_send()
        return carry

    lax.fori_loop(1, PLANE, finish_back, 0)
    for copy in stores:
        copy.wait()


def layer(exponent, query, key, value):
    anywhere = pl.BlockSpec(memory_space=pl.ANY)
    return pl.pallas_call(
        layer_kernel,
        out_shape=jax.ShapeDtypeStruct((BLOCK, D), jnp.bfloat16),
        in_specs=[
            pl.BlockSpec(memory_space=pltpu.SMEM),
            anywhere,
            anywhere,
            anywhere,
        ],
        out_specs=anywhere,
        scratch_shapes=[
            pltpu.VMEM((3, BLOCK, D), jnp.bfloat16),
            pltpu.VMEM((3, D, BLOCK), jnp.bfloat16),
            pltpu.VMEM((2, 2, BLOCK, (PAD + PLANE) * BLOCK), jnp.bfloat16),
            pltpu.VMEM((2, PLANE, HS, BLOCK), jnp.bfloat16),
            pltpu.VMEM((PLANE * BLOCK, BLOCK), jnp.bfloat16),
            pltpu.VMEM((CHAINS, ROWS, BLOCK), jnp.float32),
            pltpu.VMEM((2, PLANE, HS, BLOCK), jnp.bfloat16),
            pltpu.VMEM((D, BLOCK), jnp.bfloat16),
            pltpu.VMEM((BLOCK, D), jnp.bfloat16),
            pltpu.SemaphoreType.DMA((3, 2)),
            pltpu.SemaphoreType.DMA((PLANE, 2, 2)),
            pltpu.SemaphoreType.DMA((PLANE, 2, 2)),
            pltpu.SemaphoreType.DMA((2, 2)),
            pltpu.SemaphoreType.DMA((PLANE, 2)),
            pltpu.SemaphoreType.DMA((8 + PLANE, 2)),
            pltpu.SemaphoreType.DMA((8,)),
            pltpu.SemaphoreType.DMA((PLANE, 2)),
            pltpu.SemaphoreType.DMA((PLANE, 2)),
            pltpu.SemaphoreType.DMA((2,)),
        ],
        compiler_params=pltpu.CompilerParams(
            collective_id=0, has_side_effects=True, vmem_limit_bytes=60 << 20
        ),
        name="layer",
    )(exponent, query, key, value)


def on_device(query, key, value, exponent):
    return layer(exponent, query, key, value)


def solution(mesh):
    return jax.shard_map(
        on_device,
        mesh=mesh,
        in_specs=(
            P(("seq", "head"), None),
            P(("seq", "head"), None),
            P(("seq", "head"), None),
            P(),
        ),
        out_specs=P(("seq", "head"), None),
        check_vma=False,
    )
```

```python
import jax
import jax.numpy as jnp
from jax import lax
from jax.experimental import pallas as pl
from jax.experimental.pallas import tpu as pltpu
from jax.sharding import PartitionSpec as P

BLOCK = 128
MIN_BAND = 16
MAX_BAND = 40
HEADS = 64
HS = 112
D = HEADS * HS
HALF = D // 2
PLANE = 32
PAD = 48
TILE = 4
ROWS = TILE * BLOCK
STRIDE = 11
CHAINS = PLANE // TILE
MESH = pl.DeviceIdType.MESH
LOG2E = 1.4426950408889634
FACTOR = HS ** (-0.5)
SCALE = FACTOR * LOG2E
PARTS = (pl.ds(1, 2), pl.ds(0, 1))


def coords():
    seq = lax.axis_index("seq")
    head = lax.axis_index("head")
    x = seq // 4
    p = (seq % 4) * 8 + head
    return x, p


def device_of(x, p):
    return (x * 4 + p // 8, p % 8)


def past_six(p):
    return (p - 6) * ((p + 26) // 32)


def most_band(slot, p):
    low = (p + 6) * 24 // 63
    high = (63 - past_six(p)) * 24 // 63
    return MIN_BAND + low + slot * (high - low)


def least_band(slot, p):
    low = past_six(p) * 24 // 63
    high = (57 - p) * 24 // 63
    return MIN_BAND + low + slot * (high - low)


def head_rows(slot, p):
    head = p + slot * (HEADS - 1 - 2 * p)
    return pl.ds(pl.multiple_of(head * HS, 16), HS)


def lanes(block):
    return pl.ds(pl.multiple_of(block * BLOCK, BLOCK), BLOCK)


def flip(x):
    size = x.shape[1]
    one = (
        lax.broadcasted_iota(jnp.int32, (size, size), 0)
        == lax.broadcasted_iota(jnp.int32, (size, size), 1)
    ).astype(jnp.bfloat16)
    return lax.dot_general(
        one, x, (((1,), (1,)), ((), ())), preferred_element_type=jnp.float32
    ).astype(jnp.bfloat16)


def greet_all(x, p):
    barrier = pltpu.get_barrier_semaphore()

    def greet(d, carry):
        pl.semaphore_signal(
            barrier, inc=1, device_id=device_of(x, (p + d) % PLANE), device_id_type=MESH
        )
        return carry

    lax.fori_loop(1, PLANE, greet, 0)
    for d in range(1, 4):
        pl.semaphore_signal(
            barrier, inc=1, device_id=device_of((x + d) % 4, p), device_id_type=MESH
        )
    return barrier


def layer_kernel(
    exponent_ref,
    q_hbm,
    k_hbm,
    v_hbm,
    out_hbm,
    staged,
    turned,
    kv,
    arrived,
    queries,
    acc_ref,
    mixed,
    back,
    result_ref,
    load,
    send,
    recv,
    own,
    halo_send,
    halo_recv,
    far_send,
    back_send,
    back_recv,
    store,
):
    x, p = coords()

    def load_copy(c, half):
        columns = pl.ds(half * HALF, HALF)
        return pltpu.make_async_copy(
            (q_hbm, k_hbm, v_hbm)[c].at[:, columns], staged.at[c, :, columns], load.at[c, half]
        )

    for half in (1, 0):
        for c in (1, 2, 0):
            load_copy(c, half).start()

    barrier = greet_all(x, p)
    row = lax.broadcasted_iota(jnp.int32, (16, BLOCK), 0)
    token = lax.broadcasted_iota(jnp.int32, (16, BLOCK), 1).astype(jnp.float32)

    def absent(index, slot):
        block = index - PAD
        return (block < -PLANE * x) | (block <= -most_band(slot, p))

    def prepare():
        ones = jnp.ones((16, BLOCK), jnp.bfloat16)
        zeros = jnp.zeros((HS, BLOCK), jnp.bfloat16)
        for slot in range(2):

            def extras(step, carry):
                for part in range(8):
                    index = step * 8 + part
                    block = (index - PAD).astype(jnp.float32)
                    dead = jnp.where(absent(index, slot), 1.0, 0.0)
                    extra = jnp.where(
                        row < 3, block, jnp.where(row < 6, token, jnp.where(row < 7, dead, 0.0))
                    )
                    kv[slot, 0, HS:BLOCK, lanes(index)] = extra.astype(jnp.bfloat16)
                    kv[slot, 1, HS:BLOCK, lanes(index)] = ones
                return carry

            lax.fori_loop(0, (PAD + PLANE) // 8, extras, 0)

            def clear(index, carry):
                @pl.when(absent(index, slot))
                def _():
                    for c in range(2):
                        kv[slot, c, 0:HS, lanes(index)] = zeros

                return carry

            lax.fori_loop(0, PAD, clear, 0)

    def turn_half(half, tensors):
        def turn(step, carry):
            for part in range(7):
                at = lanes(half * 28 + step * 7 + part)
                for c in tensors:
                    turned[c, at, :] = flip(staged[c, :, at])
            return carry

        for c in tensors:
            load_copy(c, half).wait()
        lax.fori_loop(0, 4, turn, 0)

    def message(j, slot, part, place, peer, sem):
        source = turned.at[PARTS[part], head_rows(slot, place), :]
        if part == 0:
            target = kv.at[slot, :, pl.ds(0, HS), lanes(PAD + j)]
        else:
            target = arrived.at[pl.ds(slot, 1), j]
        return pltpu.make_async_remote_copy(
            src_ref=source,
            dst_ref=target,
            send_sem=send.at[sem, slot, part],
            recv_sem=recv.at[j, slot, part],
            device_id=device_of(x, peer),
            device_id_type=MESH,
        )

    def to_peer(d, slot, part):
        peer = (p + STRIDE * d) % PLANE
        return message(p, slot, part, peer, peer, d)

    def from_peer(j, slot, part):
        return message(j, slot, part, 0, (p + 1) % PLANE, 0)

    def own_copy(slot, part):
        if part == 0:
            target = kv.at[slot, :, pl.ds(0, HS), lanes(PAD + p)]
        else:
            target = arrived.at[pl.ds(slot, 1), p]
        return pltpu.make_async_copy(
            turned.at[PARTS[part], head_rows(slot, p), :], target, own.at[slot, part]
        )

    def near(j, slot):
        return pltpu.make_async_remote_copy(
            src_ref=kv.at[slot, :, pl.ds(0, HS), lanes(PAD + j)],
            dst_ref=kv.at[slot, :, pl.ds(0, HS), lanes(PAD - PLANE + j)],
            send_sem=halo_send.at[j, slot],
            recv_sem=halo_recv.at[8 + j, slot],
            device_id=device_of((x + 1) % 4, p),
            device_id_type=MESH,
        )

    def far(j):
        return pltpu.make_async_remote_copy(
            src_ref=kv.at[1, :, pl.ds(0, HS), lanes(PAD + j)],
            dst_ref=kv.at[1, :, pl.ds(0, HS), lanes(PAD - 2 * PLANE + j)],
            send_sem=far_send.at[j - 24],
            recv_sem=halo_recv.at[j - 24, 1],
            device_id=device_of((x + 2) % 4, p),
            device_id_type=MESH,
        )

    def near_needed(j, slot):
        return j >= 33 - most_band(slot, p)

    def far_needed(j):
        return (j >= 25) & (j >= 65 - most_band(1, p))

    def forward(j, slot):
        @pl.when((x < 3) & near_needed(j, slot))
        def _():
            near(j, slot).start()

        if slot == 1:

            @pl.when((x < 2) & far_needed(j))
            def _():
                far(j).start()

    def start_part(slot, part):
        def start(d, carry):
            to_peer(d, slot, part).start()
            return carry

        lax.fori_loop(1, PLANE, start, 0)
        own_copy(slot, part).start()

    turn_half(1, (1, 2))
    pl.semaphore_wait(barrier, PLANE - 1 + 3)
    start_part(1, 0)
    turn_half(1, (0,))
    start_part(1, 1)
    prepare()
    turn_half(0, (1, 2))
    own_copy(0, 0).start()

    def take(d, slot):
        j = (p + STRIDE * (PLANE - d)) % PLANE
        from_peer(j, slot, 0).wait_recv()
        forward(j, slot)

    own_copy(1, 0).wait()
    forward(p, 1)

    def take_heavy(d, carry):
        take(d, 1)
        to_peer(d, 0, 0).start()
        return carry

    lax.fori_loop(1, PLANE, take_heavy, 0)
    turn_half(0, (0,))
    own_copy(0, 1).start()

    causal = lax.broadcasted_iota(jnp.int32, (ROWS, ROWS), 1) <= lax.broadcasted_iota(
        jnp.int32, (ROWS, ROWS), 0
    )

    def send_back(block, slot):
        return pltpu.make_async_remote_copy(
            src_ref=mixed.at[slot, block],
            dst_ref=back.at[head_rows(slot, p), :],
            send_sem=back_send.at[block, slot],
            recv_sem=back_recv.at[p, slot],
            device_id=device_of(x, block),
            device_id_type=MESH,
        )

    def keep_back(slot):
        return pltpu.make_async_copy(
            mixed.at[slot, p], back.at[head_rows(slot, p), :], back_recv.at[p, slot]
        )

    def got_back(j, slot):
        return pltpu.make_async_remote_copy(
            src_ref=mixed.at[slot, 0],
            dst_ref=back.at[head_rows(slot, j), :],
            send_sem=back_send.at[0, slot],
            recv_sem=back_recv.at[j, slot],
            device_id=device_of(x, (p + 1) % PLANE),
            device_id_type=MESH,
        )

    def attend(slot):
        exponent = exponent_ref[p + slot * (HEADS - 1 - 2 * p)]
        band = MIN_BAND + (exponent - 1) * (MAX_BAND - MIN_BAND) // (HEADS - 1)
        power = jnp.full((1, BLOCK), exponent.astype(jnp.float32)) * (-12.0 / HEADS)

        own_copy(slot, 1).wait()

        def take_query(d, carry):
            from_peer((p + STRIDE * (PLANE - d)) % PLANE, slot, 1).wait_recv()
            if slot == 1:
                to_peer(d, 0, 1).start()
            return carry

        lax.fori_loop(1, PLANE, take_query, 0)
        slope = jnp.exp2(power) * (BLOCK / FACTOR)
        high = slope.astype(jnp.bfloat16).astype(jnp.float32)
        middle = (slope - high).astype(jnp.bfloat16).astype(jnp.float32)
        low = (slope - high - middle).astype(jnp.bfloat16).astype(jnp.float32)
        kind = row % 3
        parts = jnp.where(kind == 0, high, jnp.where(kind == 1, middle, low))
        parts = jnp.where(
            row < 3,
            parts,
            jnp.where(row < 6, parts * (1.0 / BLOCK), jnp.where(row < 7, -1e30, 0.0)),
        ).astype(jnp.bfloat16)

        def put_queries(step, carry):
            for part in range(8):
                index = step * 8 + part
                queries[lanes(index), :] = flip(
                    jnp.concatenate([arrived[slot, index], parts], axis=0)
                )
            return carry

        lax.fori_loop(0, PLANE // 8, put_queries, 0)

        def take_halo(n):
            for part in range(TILE):
                j = PLANE - TILE - TILE * n + part

                @pl.when((x > 0) & (j >= 0) & near_needed(j, slot))
                def _():
                    near(j, slot).wait_recv()

                if slot == 1:

                    @pl.when((x > 1) & (j < 0) & far_needed(j + PLANE))
                    def _():
                        far(j + PLANE).wait_recv()

        def scores(chain, first):
            at = pl.multiple_of((first + PAD) * BLOCK, BLOCK)
            return jnp.dot(
                queries[chain * ROWS : (chain + 1) * ROWS, :],
                kv[slot, 0, :, pl.ds(at, ROWS)],
                preferred_element_type=jnp.float32,
            )

        def mix(first, weight):
            at = pl.multiple_of((first + PAD) * BLOCK, BLOCK)
            return lax.dot_general(
                weight.astype(jnp.bfloat16),
                kv[slot, 1, :, pl.ds(at, ROWS)],
                (((1,), (1,)), ((), ())),
                preferred_element_type=jnp.float32,
            )

        def sweep(tops, offset, kind):
            starts = [c * TILE + offset for c in range(CHAINS)]

            def tile(c):
                s = scores(c, starts[c])
                if kind == "first":
                    s = jnp.where(causal, s, -1e30)
                    return s, jnp.max(s, axis=1, keepdims=True)
                if kind == "edge":
                    rows = []
                    for r in range(TILE):
                        columns = []
                        for k in range(TILE):
                            far_off = jnp.where(offset + (k - r) > -band, 0.0, -1e30)
                            columns.append(
                                s[r * BLOCK : (r + 1) * BLOCK, k * BLOCK : (k + 1) * BLOCK]
                                + far_off
                            )
                        rows.append(jnp.concatenate(columns, axis=1))
                    s = jnp.concatenate(rows, axis=0)
                return s, jnp.maximum(tops[c], jnp.max(s, axis=1, keepdims=True))

            after = []
            ready = tile(0)
            for c in range(CHAINS):
                s, new = ready
                if c + 1 < CHAINS:
                    ready = tile(c + 1)
                fresh = mix(starts[c], jnp.exp2((s - new) * SCALE))
                if kind == "first":
                    acc_ref[c] = fresh
                else:
                    acc_ref[c] = acc_ref[c] * jnp.exp2((tops[c] - new) * SCALE) + fresh
                after.append(new)
            return tuple(after)

        tops = sweep(None, 0, "first")
        if slot == 1:
            own_copy(0, 0).wait()
            forward(p, 0)
        full = (least_band(slot, p) - TILE) // TILE
        total = (most_band(slot, p) + 2) // TILE

        def inner(n, tops):
            if slot == 1:
                for part in range(7):
                    d = 1 + n * 7 + part

                    @pl.when(d < PLANE)
                    def _():
                        take(d, 0)

            take_halo(n)
            return sweep(tops, -TILE * (n + 1), "inner")

        def edge(n, tops):
            take_halo(n)
            return sweep(tops, -TILE * (n + 1), "edge")

        tops = lax.fori_loop(0, full, inner, tops)
        lax.fori_loop(full, total, edge, tops)
        for c in range(CHAINS):
            result = (acc_ref[c, :, 0:HS] / acc_ref[c, :, HS : HS + 1]).astype(jnp.bfloat16)
            for b in range(TILE):
                block = c * TILE + b
                mixed[slot, block] = flip(result[b * BLOCK : (b + 1) * BLOCK])

        def give(d, carry):
            send_back((p + STRIDE * d) % PLANE, slot).start()
            return carry

        lax.fori_loop(1, PLANE, give, 0)
        keep_back(slot).start()

    attend(1)
    attend(0)

    def unturn_half(half):
        def arrive(d, carry):
            got_back((p + STRIDE * (PLANE - d)) % PLANE, half).wait_recv()
            return carry

        keep_back(half).wait()
        lax.fori_loop(1, PLANE, arrive, 0)

        def unturn(step, carry):
            for part in range(7):
                at = lanes(half * 28 + step * 7 + part)
                result_ref[:, at] = flip(back[at, :])
            return carry

        lax.fori_loop(0, 4, unturn, 0)
        columns = pl.ds(half * HALF, HALF)
        copy = pltpu.make_async_copy(
            result_ref.at[:, columns], out_hbm.at[:, columns], store.at[half]
        )
        copy.start()
        return copy

    stores = [unturn_half(1)]

    def finish(d, carry):
        for slot in range(2):

            @pl.when(d > 0)
            def _():
                for part in range(2):
                    to_peer(d, slot, part).wait_send()

            @pl.when((x < 3) & near_needed(d, slot))
            def _():
                near(d, slot).wait_send()

        @pl.when((x < 2) & far_needed(d))
        def _():
            far(d).wait_send()

        return carry

    lax.fori_loop(0, PLANE, finish, 0)
    stores.append(unturn_half(0))

    def finish_back(d, carry):
        for slot in range(2):
            send_back((p + d) % PLANE, slot).wait_send()
        return carry

    lax.fori_loop(1, PLANE, finish_back, 0)
    for copy in stores:
        copy.wait()


def layer(exponent, query, key, value):
    anywhere = pl.BlockSpec(memory_space=pl.ANY)
    return pl.pallas_call(
        layer_kernel,
        out_shape=jax.ShapeDtypeStruct((BLOCK, D), jnp.bfloat16),
        in_specs=[
            pl.BlockSpec(memory_space=pltpu.SMEM),
            anywhere,
            anywhere,
            anywhere,
        ],
        out_specs=anywhere,
        scratch_shapes=[
            pltpu.VMEM((3, BLOCK, D), jnp.bfloat16),
            pltpu.VMEM((3, D, BLOCK), jnp.bfloat16),
            pltpu.VMEM((2, 2, BLOCK, (PAD + PLANE) * BLOCK), jnp.bfloat16),
            pltpu.VMEM((2, PLANE, HS, BLOCK), jnp.bfloat16),
            pltpu.VMEM((PLANE * BLOCK, BLOCK), jnp.bfloat16),
            pltpu.VMEM((CHAINS, ROWS, BLOCK), jnp.float32),
            pltpu.VMEM((2, PLANE, HS, BLOCK), jnp.bfloat16),
            pltpu.VMEM((D, BLOCK), jnp.bfloat16),
            pltpu.VMEM((BLOCK, D), jnp.bfloat16),
            pltpu.SemaphoreType.DMA((3, 2)),
            pltpu.SemaphoreType.DMA((PLANE, 2, 2)),
            pltpu.SemaphoreType.DMA((PLANE, 2, 2)),
            pltpu.SemaphoreType.DMA((2, 2)),
            pltpu.SemaphoreType.DMA((PLANE, 2)),
            pltpu.SemaphoreType.DMA((8 + PLANE, 2)),
            pltpu.SemaphoreType.DMA((8,)),
            pltpu.SemaphoreType.DMA((PLANE, 2)),
            pltpu.SemaphoreType.DMA((PLANE, 2)),
            pltpu.SemaphoreType.DMA((2,)),
        ],
        compiler_params=pltpu.CompilerParams(
            collective_id=0, has_side_effects=True, vmem_limit_bytes=60 << 20
        ),
        name="layer",
    )(exponent, query, key, value)


def on_device(query, key, value, exponent):
    return layer(exponent, query, key, value)


def solution(mesh):
    return jax.shard_map(
        on_device,
        mesh=mesh,
        in_specs=(
            P(("seq", "head"), None),
            P(("seq", "head"), None),
            P(("seq", "head"), None),
            P(),
        ),
        out_specs=P(("seq", "head"), None),
        check_vma=False,
    )
```

```python
import jax
import jax.numpy as jnp
from jax import lax
from jax.experimental import pallas as pl
from jax.experimental.pallas import tpu as pltpu
from jax.sharding import PartitionSpec as P

BLOCK = 128
MIN_BAND = 16
MAX_BAND = 40
HEADS = 64
HS = 112
D = HEADS * HS
HALF = D // 2
PLANE = 32
PAD = 48
TILE = 4
ROWS = TILE * BLOCK
STRIDE = 11
CHAINS = PLANE // TILE
MESH = pl.DeviceIdType.MESH
LOG2E = 1.4426950408889634
FACTOR = HS ** (-0.5)
SCALE = FACTOR * LOG2E
PARTS = (pl.ds(1, 2), pl.ds(0, 1))


def coords():
    seq = lax.axis_index("seq")
    head = lax.axis_index("head")
    x = seq // 4
    p = (seq % 4) * 8 + head
    return x, p


def device_of(x, p):
    return (x * 4 + p // 8, p % 8)


def past_six(p):
    return (p - 6) * ((p + 26) // 32)


def most_band(slot, p):
    low = (p + 6) * 24 // 63
    high = (63 - past_six(p)) * 24 // 63
    return MIN_BAND + low + slot * (high - low)


def least_band(slot, p):
    low = past_six(p) * 24 // 63
    high = (57 - p) * 24 // 63
    return MIN_BAND + low + slot * (high - low)


def head_rows(slot, p):
    head = p + slot * (HEADS - 1 - 2 * p)
    return pl.ds(pl.multiple_of(head * HS, 16), HS)


def lanes(block):
    return pl.ds(pl.multiple_of(block * BLOCK, BLOCK), BLOCK)


def flip(x):
    size = x.shape[1]
    one = (
        lax.broadcasted_iota(jnp.int32, (size, size), 0)
        == lax.broadcasted_iota(jnp.int32, (size, size), 1)
    ).astype(jnp.bfloat16)
    return lax.dot_general(
        one, x, (((1,), (1,)), ((), ())), preferred_element_type=jnp.float32
    ).astype(jnp.bfloat16)


def greet_all(x, p):
    barrier = pltpu.get_barrier_semaphore()

    def greet(d, carry):
        pl.semaphore_signal(
            barrier, inc=1, device_id=device_of(x, (p + d) % PLANE), device_id_type=MESH
        )
        return carry

    lax.fori_loop(1, PLANE, greet, 0)
    for d in range(1, 4):
        pl.semaphore_signal(
            barrier, inc=1, device_id=device_of((x + d) % 4, p), device_id_type=MESH
        )
    return barrier


def layer_kernel(
    exponent_ref,
    q_hbm,
    k_hbm,
    v_hbm,
    out_hbm,
    staged,
    turned,
    kv,
    arrived,
    queries,
    acc_ref,
    mixed,
    back,
    result_ref,
    load,
    send,
    recv,
    own,
    halo_send,
    halo_recv,
    far_send,
    back_send,
    back_recv,
    store,
):
    x, p = coords()

    def load_copy(c, half):
        columns = pl.ds(half * HALF, HALF)
        return pltpu.make_async_copy(
            (q_hbm, k_hbm, v_hbm)[c].at[:, columns], staged.at[c, :, columns], load.at[c, half]
        )

    for half in (1, 0):
        for c in (1, 2, 0):
            load_copy(c, half).start()

    barrier = greet_all(x, p)
    row = lax.broadcasted_iota(jnp.int32, (16, BLOCK), 0)
    token = lax.broadcasted_iota(jnp.int32, (16, BLOCK), 1).astype(jnp.float32)

    def absent(index, slot):
        block = index - PAD
        return (block < -PLANE * x) | (block <= -most_band(slot, p))

    def prepare(d):
        for slot in range(2):
            for part in range(3):
                index = 3 * (d - 1) + part

                @pl.when(index < PAD + PLANE)
                def _():
                    block = (index - PAD).astype(jnp.float32)
                    dead = jnp.where(absent(index, slot), 1.0, 0.0)
                    extra = jnp.where(
                        row < 3, block, jnp.where(row < 6, token, jnp.where(row < 7, dead, 0.0))
                    )
                    kv[slot, 0, HS:BLOCK, lanes(index)] = extra.astype(jnp.bfloat16)
                    kv[slot, 1, HS:BLOCK, lanes(index)] = jnp.ones((16, BLOCK), jnp.bfloat16)

            for part in range(2):
                index = 2 * (d - 1) + part

                @pl.when((index < PAD) & absent(index, slot))
                def _():
                    for c in range(2):
                        kv[slot, c, 0:HS, lanes(index)] = jnp.zeros((HS, BLOCK), jnp.bfloat16)

    def turn_half(half, tensors):
        def turn(step, carry):
            for part in range(7):
                at = lanes(half * 28 + step * 7 + part)
                for c in tensors:
                    turned[c, at, :] = flip(staged[c, :, at])
            return carry

        for c in tensors:
            load_copy(c, half).wait()
        lax.fori_loop(0, 4, turn, 0)

    def message(j, slot, part, place, peer, sem):
        source = turned.at[PARTS[part], head_rows(slot, place), :]
        if part == 0:
            target = kv.at[slot, :, pl.ds(0, HS), lanes(PAD + j)]
        else:
            target = arrived.at[pl.ds(slot, 1), j]
        return pltpu.make_async_remote_copy(
            src_ref=source,
            dst_ref=target,
            send_sem=send.at[sem, slot, part],
            recv_sem=recv.at[j, slot, part],
            device_id=device_of(x, peer),
            device_id_type=MESH,
        )

    def to_peer(d, slot, part):
        peer = (p + STRIDE * d) % PLANE
        return message(p, slot, part, peer, peer, d)

    def from_peer(j, slot, part):
        return message(j, slot, part, 0, (p + 1) % PLANE, 0)

    def own_copy(slot, part):
        if part == 0:
            target = kv.at[slot, :, pl.ds(0, HS), lanes(PAD + p)]
        else:
            target = arrived.at[pl.ds(slot, 1), p]
        return pltpu.make_async_copy(
            turned.at[PARTS[part], head_rows(slot, p), :], target, own.at[slot, part]
        )

    def near(j, slot):
        return pltpu.make_async_remote_copy(
            src_ref=kv.at[slot, :, pl.ds(0, HS), lanes(PAD + j)],
            dst_ref=kv.at[slot, :, pl.ds(0, HS), lanes(PAD - PLANE + j)],
            send_sem=halo_send.at[j, slot],
            recv_sem=halo_recv.at[8 + j, slot],
            device_id=device_of((x + 1) % 4, p),
            device_id_type=MESH,
        )

    def far(j):
        return pltpu.make_async_remote_copy(
            src_ref=kv.at[1, :, pl.ds(0, HS), lanes(PAD + j)],
            dst_ref=kv.at[1, :, pl.ds(0, HS), lanes(PAD - 2 * PLANE + j)],
            send_sem=far_send.at[j - 24],
            recv_sem=halo_recv.at[j - 24, 1],
            device_id=device_of((x + 2) % 4, p),
            device_id_type=MESH,
        )

    def near_needed(j, slot):
        return j >= 33 - most_band(slot, p)

    def far_needed(j):
        return (j >= 25) & (j >= 65 - most_band(1, p))

    def forward(j, slot):
        @pl.when((x < 3) & near_needed(j, slot))
        def _():
            near(j, slot).start()

        if slot == 1:

            @pl.when((x < 2) & far_needed(j))
            def _():
                far(j).start()

    def start_part(slot, part):
        def start(d, carry):
            to_peer(d, slot, part).start()
            return carry

        lax.fori_loop(1, PLANE, start, 0)
        own_copy(slot, part).start()

    turn_half(1, (1, 2))
    pl.semaphore_wait(barrier, PLANE - 1 + 3)
    start_part(1, 0)
    turn_half(1, (0,))
    start_part(1, 1)

    def take(d, slot):
        j = (p + STRIDE * (PLANE - d)) % PLANE
        from_peer(j, slot, 0).wait_recv()
        forward(j, slot)

    own_copy(1, 0).wait()
    forward(p, 1)

    for c in (1, 2):
        load_copy(c, 0).wait()

    def take_heavy(d, carry):
        take(d, 1)

        @pl.when(d <= 28)
        def _():
            at = lanes(d - 1)
            for c in (1, 2):
                turned[c, at, :] = flip(staged[c, :, at])

        prepare(d)
        return carry

    lax.fori_loop(1, PLANE, take_heavy, 0)
    own_copy(0, 0).start()
    turn_half(0, (0,))
    own_copy(0, 1).start()

    causal = lax.broadcasted_iota(jnp.int32, (ROWS, ROWS), 1) <= lax.broadcasted_iota(
        jnp.int32, (ROWS, ROWS), 0
    )

    def send_back(block, slot):
        return pltpu.make_async_remote_copy(
            src_ref=mixed.at[slot, block],
            dst_ref=back.at[head_rows(slot, p), :],
            send_sem=back_send.at[block, slot],
            recv_sem=back_recv.at[p, slot],
            device_id=device_of(x, block),
            device_id_type=MESH,
        )

    def keep_back(slot):
        return pltpu.make_async_copy(
            mixed.at[slot, p], back.at[head_rows(slot, p), :], back_recv.at[p, slot]
        )

    def got_back(j, slot):
        return pltpu.make_async_remote_copy(
            src_ref=mixed.at[slot, 0],
            dst_ref=back.at[head_rows(slot, j), :],
            send_sem=back_send.at[0, slot],
            recv_sem=back_recv.at[j, slot],
            device_id=device_of(x, (p + 1) % PLANE),
            device_id_type=MESH,
        )

    def attend(slot):
        exponent = exponent_ref[p + slot * (HEADS - 1 - 2 * p)]
        band = MIN_BAND + (exponent - 1) * (MAX_BAND - MIN_BAND) // (HEADS - 1)
        power = jnp.full((1, BLOCK), exponent.astype(jnp.float32)) * (-12.0 / HEADS)

        own_copy(slot, 1).wait()

        def take_query(d, carry):
            from_peer((p + STRIDE * (PLANE - d)) % PLANE, slot, 1).wait_recv()
            if slot == 1:
                to_peer(d, 0, 0).start()
            return carry

        lax.fori_loop(1, PLANE, take_query, 0)
        if slot == 1:

            def ask(d, carry):
                to_peer(d, 0, 1).start()
                return carry

            lax.fori_loop(1, PLANE, ask, 0)
        slope = jnp.exp2(power) * (BLOCK / FACTOR)
        high = slope.astype(jnp.bfloat16).astype(jnp.float32)
        middle = (slope - high).astype(jnp.bfloat16).astype(jnp.float32)
        low = (slope - high - middle).astype(jnp.bfloat16).astype(jnp.float32)
        kind = row % 3
        parts = jnp.where(kind == 0, high, jnp.where(kind == 1, middle, low))
        parts = jnp.where(
            row < 3,
            parts,
            jnp.where(row < 6, parts * (1.0 / BLOCK), jnp.where(row < 7, -1e30, 0.0)),
        ).astype(jnp.bfloat16)

        def put_queries(step, carry):
            for part in range(8):
                index = step * 8 + part
                queries[lanes(index), :] = flip(
                    jnp.concatenate([arrived[slot, index], parts], axis=0)
                )
            return carry

        lax.fori_loop(0, PLANE // 8, put_queries, 0)

        def take_halo(n):
            for part in range(TILE):
                j = PLANE - TILE - TILE * n + part

                @pl.when((x > 0) & (j >= 0) & near_needed(j, slot))
                def _():
                    near(j, slot).wait_recv()

                if slot == 1:

                    @pl.when((x > 1) & (j < 0) & far_needed(j + PLANE))
                    def _():
                        far(j + PLANE).wait_recv()

        def scores(chain, first):
            at = pl.multiple_of((first + PAD) * BLOCK, BLOCK)
            return jnp.dot(
                queries[chain * ROWS : (chain + 1) * ROWS, :],
                kv[slot, 0, :, pl.ds(at, ROWS)],
                preferred_element_type=jnp.float32,
            )

        def mix(first, weight):
            at = pl.multiple_of((first + PAD) * BLOCK, BLOCK)
            return lax.dot_general(
                weight.astype(jnp.bfloat16),
                kv[slot, 1, :, pl.ds(at, ROWS)],
                (((1,), (1,)), ((), ())),
                preferred_element_type=jnp.float32,
            )

        def sweep(tops, offset, kind):
            starts = [c * TILE + offset for c in range(CHAINS)]

            def tile(c):
                s = scores(c, starts[c])
                if kind == "first":
                    s = jnp.where(causal, s, -1e30)
                    return s, jnp.max(s, axis=1, keepdims=True)
                if kind == "edge":
                    rows = []
                    for r in range(TILE):
                        columns = []
                        for k in range(TILE):
                            far_off = jnp.where(offset + (k - r) > -band, 0.0, -1e30)
                            columns.append(
                                s[r * BLOCK : (r + 1) * BLOCK, k * BLOCK : (k + 1) * BLOCK]
                                + far_off
                            )
                        rows.append(jnp.concatenate(columns, axis=1))
                    s = jnp.concatenate(rows, axis=0)
                return s, jnp.maximum(tops[c], jnp.max(s, axis=1, keepdims=True))

            after = []
            ready = tile(0)
            for c in range(CHAINS):
                s, new = ready
                if c + 1 < CHAINS:
                    ready = tile(c + 1)
                fresh = mix(starts[c], jnp.exp2((s - new) * SCALE))
                if kind == "first":
                    acc_ref[c] = fresh
                else:
                    acc_ref[c] = acc_ref[c] * jnp.exp2((tops[c] - new) * SCALE) + fresh
                after.append(new)
            return tuple(after)

        tops = sweep(None, 0, "first")
        if slot == 1:
            own_copy(0, 0).wait()
            forward(p, 0)
        full = (least_band(slot, p) - TILE) // TILE
        total = (most_band(slot, p) + 2) // TILE

        def inner(n, tops):
            if slot == 1:
                for part in range(7):
                    d = 1 + n * 7 + part

                    @pl.when(d < PLANE)
                    def _():
                        take(d, 0)

            take_halo(n)
            return sweep(tops, -TILE * (n + 1), "inner")

        def edge(n, tops):
            take_halo(n)
            return sweep(tops, -TILE * (n + 1), "edge")

        tops = lax.fori_loop(0, full, inner, tops)
        lax.fori_loop(full, total, edge, tops)
        for c in range(CHAINS):
            result = (acc_ref[c, :, 0:HS] / acc_ref[c, :, HS : HS + 1]).astype(jnp.bfloat16)
            for b in range(TILE):
                block = c * TILE + b
                mixed[slot, block] = flip(result[b * BLOCK : (b + 1) * BLOCK])

        def give(d, carry):
            send_back((p + STRIDE * d) % PLANE, slot).start()
            return carry

        lax.fori_loop(1, PLANE, give, 0)
        keep_back(slot).start()

    attend(1)
    attend(0)

    def unturn_half(half):
        def arrive(d, carry):
            got_back((p + STRIDE * (PLANE - d)) % PLANE, half).wait_recv()
            return carry

        keep_back(half).wait()
        lax.fori_loop(1, PLANE, arrive, 0)

        def unturn(step, carry):
            for part in range(7):
                at = lanes(half * 28 + step * 7 + part)
                result_ref[:, at] = flip(back[at, :])
            return carry

        lax.fori_loop(0, 4, unturn, 0)
        columns = pl.ds(half * HALF, HALF)
        copy = pltpu.make_async_copy(
            result_ref.at[:, columns], out_hbm.at[:, columns], store.at[half]
        )
        copy.start()
        return copy

    stores = [unturn_half(1)]

    def finish(d, carry):
        for slot in range(2):

            @pl.when(d > 0)
            def _():
                for part in range(2):
                    to_peer(d, slot, part).wait_send()

            @pl.when((x < 3) & near_needed(d, slot))
            def _():
                near(d, slot).wait_send()

        @pl.when((x < 2) & far_needed(d))
        def _():
            far(d).wait_send()

        return carry

    lax.fori_loop(0, PLANE, finish, 0)
    stores.append(unturn_half(0))

    def finish_back(d, carry):
        for slot in range(2):
            send_back((p + d) % PLANE, slot).wait_send()
        return carry

    lax.fori_loop(1, PLANE, finish_back, 0)
    for copy in stores:
        copy.wait()


def layer(exponent, query, key, value):
    anywhere = pl.BlockSpec(memory_space=pl.ANY)
    return pl.pallas_call(
        layer_kernel,
        out_shape=jax.ShapeDtypeStruct((BLOCK, D), jnp.bfloat16),
        in_specs=[
            pl.BlockSpec(memory_space=pltpu.SMEM),
            anywhere,
            anywhere,
            anywhere,
        ],
        out_specs=anywhere,
        scratch_shapes=[
            pltpu.VMEM((3, BLOCK, D), jnp.bfloat16),
            pltpu.VMEM((3, D, BLOCK), jnp.bfloat16),
            pltpu.VMEM((2, 2, BLOCK, (PAD + PLANE) * BLOCK), jnp.bfloat16),
            pltpu.VMEM((2, PLANE, HS, BLOCK), jnp.bfloat16),
            pltpu.VMEM((PLANE * BLOCK, BLOCK), jnp.bfloat16),
            pltpu.VMEM((CHAINS, ROWS, BLOCK), jnp.float32),
            pltpu.VMEM((2, PLANE, HS, BLOCK), jnp.bfloat16),
            pltpu.VMEM((D, BLOCK), jnp.bfloat16),
            pltpu.VMEM((BLOCK, D), jnp.bfloat16),
            pltpu.SemaphoreType.DMA((3, 2)),
            pltpu.SemaphoreType.DMA((PLANE, 2, 2)),
            pltpu.SemaphoreType.DMA((PLANE, 2, 2)),
            pltpu.SemaphoreType.DMA((2, 2)),
            pltpu.SemaphoreType.DMA((PLANE, 2)),
            pltpu.SemaphoreType.DMA((8 + PLANE, 2)),
            pltpu.SemaphoreType.DMA((8,)),
            pltpu.SemaphoreType.DMA((PLANE, 2)),
            pltpu.SemaphoreType.DMA((PLANE, 2)),
            pltpu.SemaphoreType.DMA((2,)),
        ],
        compiler_params=pltpu.CompilerParams(
            collective_id=0, has_side_effects=True, vmem_limit_bytes=60 << 20
        ),
        name="layer",
    )(exponent, query, key, value)


def on_device(query, key, value, exponent):
    return layer(exponent, query, key, value)


def solution(mesh):
    return jax.shard_map(
        on_device,
        mesh=mesh,
        in_specs=(
            P(("seq", "head"), None),
            P(("seq", "head"), None),
            P(("seq", "head"), None),
            P(),
        ),
        out_specs=P(("seq", "head"), None),
        check_vma=False,
    )
```
